256 devices in a mesh: dp: 8 (over z), own: 32 (over x, y, core).
Axes of the slice: x: 4, y: 4, z: 8, core: 2. Of those that a mesh axis runs over, the one named last changes fastest.
Arguments:
- signals: bfloat16 [65536, 384], P(('dp', 'own')), may hold values from -6 to 6
- cotangent: bfloat16 [65536, 384], P(('dp', 'own')), may hold values from -6 to 6
- row_insertion: int32 [65536], P(('dp', 'own')), may hold values from 0 to 63, as said below
- touched: int32 [256, 4], replicated, may hold values from 0 to 63, as said below
- slot_map: int32 [64], replicated, may hold values from 0 to 63, each once
- weights: bfloat16 [64, 2, 384, 1024], P(None, None, 'own'), may hold values from -0.3125 to 0.3125
- moment1: float32 [64, 2, 384, 1024], P(None, None, 'own', 'dp'), may hold values from -25.6 to 25.6
- moment2: float32 [64, 2, 384, 1024], P(None, None, 'own', 'dp'), may hold values from 0.2048 to 6.144
Outputs:
- predicted: bfloat16 [65536, 384], P(('dp', 'own'))
- new_weights: bfloat16 [64, 2, 384, 1024], P(None, None, 'own')
- new_moment1: float32 [64, 2, 384, 1024], P(None, None, 'own', 'dp')
- new_moment2: float32 [64, 2, 384, 1024], P(None, None, 'own', 'dp')
The draws below stay inside these ranges and needn't reach their ends.
Inputs may be any that keep to these rules, and one draw needn't show every extreme that they name: `row_insertion`: device d (dp index times the size of own plus own index) holds rows d * 256 to (d + 1) * 256 - 1; their insertions are all in row d of touched; at most 128 rows of one device name the same insertion, and on every device one insertion is named by exactly 128 rows. `touched`: each row lists 4 different insertions.
All inputs are finite; a program needn't handle non-finite values.
Results may differ from the reference program's by a relative error of at most 0.0049.
Values may be sent and summed in bfloat16 or wider, within the bound.
A program may use at most 128 MiB of HBM per device.

```python
import math
import jax
import jax.numpy as jnp
from jax import lax

SITES = 384
WIDTH = 1024
ROWS_DEV = 256
TOUCH = 4
CAP = 128
INSERTIONS = 64
ROWS = 65536
ROWS_INS = 1024


def listed_insertions(key):
    base = jax.random.fold_in(key, 11)
    number = ROWS // ROWS_DEV
    subkeys = jax.random.split(base, number)

    def pick(subkey):
        return jax.random.permutation(subkey, INSERTIONS)[:TOUCH]
    return jax.vmap(pick)(subkeys).astype(jnp.int32)


def draw_touched(key, part):
    return listed_insertions(key)


def draw_row_insertion(key, part):
    listed = listed_insertions(key)
    number = listed.shape[0]
    subkeys = jax.random.split(jax.random.fold_in(key, 23), number)

    def device_rows(subkey, picks):
        key_cut, key_rot, key_mix = jax.random.split(subkey, 3)
        cut_points = jax.random.randint(key_cut, (2,), 1, CAP)
        lower = jnp.min(cut_points)
        upper = jnp.max(cut_points)
        counts = jnp.stack([jnp.array(CAP, jnp.int32), lower, upper - lower, CAP - upper]).astype(jnp.int32)
        rotation = jax.random.randint(key_rot, (), 0, 4)
        counts = counts[(jnp.arange(4) - rotation) % 4]
        bounds = jnp.cumsum(counts)
        slot_rows = jnp.sum((jnp.arange(ROWS_DEV)[:, None] >= bounds[None, :]).astype(jnp.int32), axis=1)
        shuffle = jax.random.permutation(key_mix, ROWS_DEV)
        return picks[slot_rows[shuffle]]
    return jax.vmap(device_rows)(subkeys, listed).reshape(-1).astype(jnp.int32)


def block_scale(rng, dims, pieces, least, top_value):
    loudness, own = 1.0, jax.random.fold_in(rng, 6)
    for position, shards_of in pieces:
        steps = jnp.exp(jax.random.uniform(jax.random.fold_in(own, position), (shards_of,), jnp.float32, least / len(pieces), top_value / len(pieces)))
        loudness = loudness * jnp.repeat(steps, dims[position] // shards_of).reshape([-1 if axis == position else 1 for axis in range(len(dims))])
    return loudness


def noise(rng, extent, scale, limit, cuts=(), kind=jnp.bfloat16):
    loudness = block_scale(rng, extent, cuts, -0.22, 0.18) if cuts else 1.0
    values = jax.random.normal(rng, extent, jnp.float32) * scale * loudness
    return jnp.minimum(jnp.maximum(values, -limit), limit).astype(kind)


def setup_inputs(seed: int = 0) -> dict:
    streams_of = jax.random.split(jax.random.key(seed), 9)
    return {
        "signals": noise(streams_of[0], (ROWS, SITES), 1.0, 6.0, ((0, 256),)),
        "cotangent": noise(streams_of[1], (ROWS, SITES), 1.0, 6.0, ((0, 256),)),
        "row_insertion": draw_row_insertion(jax.random.fold_in(streams_of[8], 71), 0),
        "touched": draw_touched(jax.random.fold_in(streams_of[8], 71), 0),
        "slot_map": jax.random.permutation(streams_of[4], INSERTIONS).astype(jnp.int32),
        "weights": noise(streams_of[5], (INSERTIONS, 2, SITES, WIDTH), SITES ** -0.5, 0.3125, ((2, 32),)),
        "moment1": noise(streams_of[6], (INSERTIONS, 2, SITES, WIDTH), (0.2 * ROWS_INS ** 0.5), 25.6, ((2, 32), (3, 8)), jnp.float32),
        "moment2": jnp.clip(jnp.exp(math.log(6.144) - 3.4011974 * jax.random.uniform(streams_of[7], (INSERTIONS, 2, SITES, WIDTH), jnp.float32) ** block_scale(streams_of[7], (INSERTIONS, 2, SITES, WIDTH), ((2, 32), (3, 8)), -0.2, 0.2)), 0.2048, 6.144),
    }


gelu_coef = math.sqrt(2.0 / math.pi)
cubic_coef = 0.044715
learn_rate = 0.01
highest = lax.Precision.HIGHEST

def gelu_parts(preact):
    tanh_input = gelu_coef * (preact + cubic_coef * preact * preact * preact)
    tangent = jnp.tanh(tanh_input)
    gelu_val = 0.5 * preact * (1.0 + tangent)
    slopes = 0.5 * (1.0 + tangent) + 0.5 * preact * (1.0 - tangent * tangent) * gelu_coef * (1.0 + 3.0 * cubic_coef * preact * preact)
    return (gelu_val, slopes)

def dispatch(row_ids, listed):
    match_table = (row_ids[:, None] == listed[None, :]).astype(jnp.int32)
    running = jnp.cumsum(match_table, axis=0) - 1
    slot_of = lax.optimization_barrier(jnp.sum(match_table * jnp.arange(listed.shape[0], dtype=jnp.int32)[None, :], axis=1))
    within = lax.optimization_barrier(jnp.sum(match_table * running, axis=1))
    return (slot_of * CAP + within).astype(jnp.int32)

def adam_step(params, moment_one, moment_two, gradient):
    moment_one = 0.9 * moment_one + 0.1 * gradient
    moment_two = 0.999 * moment_two + 0.001 * gradient * gradient
    correct_one = 1.0 - 0.9 ** 10
    correct_two = 1.0 - 0.999 ** 10
    updated = params - learn_rate * (moment_one / correct_one) / (jnp.sqrt(moment_two / correct_two) + 1e-08)
    return (updated.astype(jnp.bfloat16), moment_one, moment_two)

def reference(signals, cotangent, row_insertion, touched, slot_map, weights, moment1, moment2):
    blocks = weights[slot_map]
    number = touched.shape[0]
    sig_dev = signals.reshape(number, ROWS_DEV, SITES)
    cot_dev = cotangent.reshape(number, ROWS_DEV, SITES)
    ids_dev = row_insertion.reshape(number, ROWS_DEV)

    def device_step(totals, inputs):
        sig_rows, cot_rows, row_ids, listed = inputs
        places = dispatch(row_ids, listed)
        stacked = jnp.zeros((TOUCH * CAP, 2 * SITES), signals.dtype).at[places].set(jnp.concatenate([sig_rows, cot_rows], axis=1))
        stacked = stacked.reshape(TOUCH, CAP, 2 * SITES).astype(jnp.float32)
        sig_slots = stacked[:, :, :SITES]
        cot_slots = stacked[:, :, SITES:]
        chosen = blocks[listed].astype(jnp.float32)
        read_in = chosen[:, 0]
        read_out = chosen[:, 1]
        preact = jnp.einsum('kcs,ksw->kcw', sig_slots, read_in, precision=highest)
        gelu_val, slopes = gelu_parts(preact)
        hidden = lax.optimization_barrier(gelu_val.astype(jnp.bfloat16)).astype(jnp.float32)
        pred_slots = jnp.einsum('kcw,ksw->kcs', hidden, read_out, precision=highest).astype(jnp.bfloat16)
        back_hidden = jnp.einsum('kcs,ksw->kcw', cot_slots, read_out, precision=highest)
        back_pre = lax.optimization_barrier((back_hidden * slopes).astype(jnp.bfloat16)).astype(jnp.float32)
        grad_in = jnp.einsum('kcs,kcw->ksw', sig_slots, back_pre, precision=highest)
        grad_out = jnp.einsum('kcs,kcw->ksw', cot_slots, hidden, precision=highest)
        totals = totals.at[listed].add(jnp.stack([grad_in, grad_out], axis=1))
        predicted = pred_slots.reshape(TOUCH * CAP, SITES)[places]
        return (totals, predicted)
    totals, predicted = lax.scan(device_step, jnp.zeros(weights.shape, jnp.float32), (sig_dev, cot_dev, ids_dev, touched))
    gradient = jnp.zeros(weights.shape, jnp.float32).at[slot_map].set(totals)
    new_weights, new_moment1, new_moment2 = adam_step(weights.astype(jnp.float32), moment1, moment2, gradient)
    return (predicted.reshape(-1, SITES), new_weights, new_moment1, new_moment2)
```

```python
import math

import jax
import jax.numpy as jnp
from jax import lax
from jax.sharding import PartitionSpec as P

SITES = 384
WIDTH = 1024
TOUCH = 4
CAP = 128


gelu_coef = math.sqrt(2.0 / math.pi)
cubic_coef = 0.044715
learn_rate = 0.01
highest = lax.Precision.HIGHEST


def gelu_parts(preact):
    tanh_input = gelu_coef * (preact + cubic_coef * preact * preact * preact)
    tangent = jnp.tanh(tanh_input)
    gelu_val = 0.5 * preact * (1.0 + tangent)
    slopes = 0.5 * (1.0 + tangent) + 0.5 * preact * (1.0 - tangent * tangent) * gelu_coef * (
        1.0 + 3.0 * cubic_coef * preact * preact
    )
    return (gelu_val, slopes)


def dispatch(row_ids, listed):
    match_table = (row_ids[:, None] == listed[None, :]).astype(jnp.int32)
    running = jnp.cumsum(match_table, axis=0) - 1
    slot_of = jnp.sum(match_table * jnp.arange(listed.shape[0], dtype=jnp.int32)[None, :], axis=1)
    within = jnp.sum(match_table * running, axis=1)
    return slot_of * CAP + within


def adam_step(params, moment_one, moment_two, gradient):
    moment_one = 0.9 * moment_one + 0.1 * gradient
    moment_two = 0.999 * moment_two + 0.001 * gradient * gradient
    correct_one = 1.0 - 0.9**10
    correct_two = 1.0 - 0.999**10
    updated = params - learn_rate * (moment_one / correct_one) / (
        jnp.sqrt(moment_two / correct_two) + 1e-08
    )
    return (updated.astype(jnp.bfloat16), moment_one, moment_two)


def sum_by_insertion(item_rows, arrived_grad, number):
    one_hot = (jnp.arange(number, dtype=jnp.int32)[:, None] == item_rows[None, :]).astype(
        arrived_grad.dtype
    )
    flat_grad = arrived_grad.reshape(item_rows.shape[0], -1)
    return jnp.dot(one_hot, flat_grad, preferred_element_type=jnp.float32)


def shards(signals, cotangent, row_insertion, touched, slot_map, weights, moment1, moment2):
    n_own = lax.axis_size("own")
    n_dp = lax.axis_size("dp")
    dp_at = lax.axis_index("dp")
    own_at = lax.axis_index("own")
    number = weights.shape[0]
    piece_rows = weights.shape[2]
    width_part = moment1.shape[3]
    stored = jnp.sum(
        jnp.where(
            touched[:, :, None] == jnp.arange(number, dtype=jnp.int32)[None, None, :],
            slot_map[None, None, :],
            0,
        ),
        axis=2,
    )
    stored_all = stored.reshape(n_dp, n_own, TOUCH)
    group_rows = lax.dynamic_index_in_dim(stored_all, dp_at, 0, keepdims=False)
    flat_rows = group_rows.reshape(-1)
    my_list = lax.dynamic_index_in_dim(touched, dp_at * n_own + own_at, 0, keepdims=False)
    places = dispatch(row_insertion, my_list)
    stacked = (
        jnp.zeros((TOUCH * CAP, 2 * SITES), signals.dtype)
        .at[places]
        .set(jnp.concatenate([signals, cotangent], axis=1))
    )
    stacked = stacked.reshape(TOUCH, CAP, 2 * SITES)
    sig_slots = stacked[:, :, :SITES]
    cot_slots = stacked[:, :, SITES:]
    read_out = None
    outgoing = jnp.take(weights, flat_rows, axis=0).reshape(n_own, TOUCH, 2, piece_rows, WIDTH)
    arrived = lax.all_to_all(outgoing, "own", split_axis=0, concat_axis=3, tiled=True)
    read_in = arrived[0, :, 0]
    read_out = arrived[0, :, 1]
    preact = jnp.einsum("kcs,ksw->kcw", sig_slots, read_in, preferred_element_type=jnp.float32)
    gelu_val, slopes = gelu_parts(preact)
    hidden = gelu_val.astype(jnp.bfloat16)
    pred_slots = jnp.einsum(
        "kcw,ksw->kcs", hidden, read_out, preferred_element_type=jnp.float32
    ).astype(jnp.bfloat16)
    back_hidden = jnp.einsum(
        "kcs,ksw->kcw", cot_slots, read_out, preferred_element_type=jnp.float32
    )
    back_pre = (back_hidden * slopes).astype(jnp.bfloat16)
    grad_in = jnp.einsum("kcs,kcw->ksw", sig_slots, back_pre, preferred_element_type=jnp.float32)
    grad_out = jnp.einsum("kcs,kcw->ksw", cot_slots, hidden, preferred_element_type=jnp.float32)
    grads = jnp.stack([grad_in, grad_out], axis=1).astype(jnp.bfloat16)
    arrived_grad = lax.all_to_all(
        lax.all_to_all(grads[None, None], "dp", split_axis=5, concat_axis=0, tiled=True),
        "own",
        split_axis=4,
        concat_axis=1,
        tiled=True,
    )
    table = sum_by_insertion(stored.reshape(-1), arrived_grad, number).reshape(
        number, 2, piece_rows, width_part
    )
    own_params = lax.dynamic_slice_in_dim(weights, dp_at * width_part, width_part, 3).astype(
        jnp.float32
    )
    fresh_part, new_moment1, new_moment2 = adam_step(own_params, moment1, moment2, table)
    new_weights = lax.all_gather(fresh_part, "dp", axis=3, tiled=True)
    predicted = pred_slots.reshape(TOUCH * CAP, SITES)[places]
    return (predicted, new_weights, new_moment1, new_moment2)


def solution(mesh):
    in_specs = (
        P(("dp", "own"), None),
        P(("dp", "own"), None),
        P(("dp", "own")),
        P(),
        P(),
        P(None, None, "own", None),
        P(None, None, "own", "dp"),
        P(None, None, "own", "dp"),
    )
    out_specs = (
        P(("dp", "own"), None),
        P(None, None, "own", None),
        P(None, None, "own", "dp"),
        P(None, None, "own", "dp"),
    )
    return jax.shard_map(shards, mesh=mesh, in_specs=in_specs, out_specs=out_specs, check_vma=False)
```

```python
import math

import jax
import jax.numpy as jnp
from jax import lax
from jax.sharding import PartitionSpec as P

SITES = 384
WIDTH = 1024
TOUCH = 4
CAP = 128


gelu_coef = math.sqrt(2.0 / math.pi)
cubic_coef = 0.044715
learn_rate = 0.01
highest = lax.Precision.HIGHEST


def gelu_parts(preact):
    tanh_input = gelu_coef * (preact + cubic_coef * preact * preact * preact)
    tangent = jnp.tanh(tanh_input)
    gelu_val = 0.5 * preact * (1.0 + tangent)
    slopes = 0.5 * (1.0 + tangent) + 0.5 * preact * (1.0 - tangent * tangent) * gelu_coef * (
        1.0 + 3.0 * cubic_coef * preact * preact
    )
    return (gelu_val, slopes)


def dispatch(row_ids, listed):
    match_table = (row_ids[:, None] == listed[None, :]).astype(jnp.int32)
    running = jnp.cumsum(match_table, axis=0) - 1
    slot_of = jnp.sum(match_table * jnp.arange(listed.shape[0], dtype=jnp.int32)[None, :], axis=1)
    within = jnp.sum(match_table * running, axis=1)
    return slot_of * CAP + within


def adam_step(params, moment_one, moment_two, gradient):
    moment_one = 0.9 * moment_one + 0.1 * gradient
    moment_two = 0.999 * moment_two + 0.001 * gradient * gradient
    correct_one = 1.0 - 0.9**10
    correct_two = 1.0 - 0.999**10
    updated = params - learn_rate * (moment_one / correct_one) / (
        jnp.sqrt(moment_two / correct_two) + 1e-08
    )
    return (updated.astype(jnp.bfloat16), moment_one, moment_two)


def sum_by_insertion(item_rows, arrived_grad, number):
    one_hot = (jnp.arange(number, dtype=jnp.int32)[:, None] == item_rows[None, :]).astype(
        arrived_grad.dtype
    )
    flat_grad = arrived_grad.reshape(item_rows.shape[0], -1)
    return jnp.dot(one_hot, flat_grad, preferred_element_type=jnp.float32)


def shards(signals, cotangent, row_insertion, touched, slot_map, weights, moment1, moment2):
    n_own = lax.axis_size("own")
    n_dp = lax.axis_size("dp")
    dp_at = lax.axis_index("dp")
    own_at = lax.axis_index("own")
    number = weights.shape[0]
    piece_rows = weights.shape[2]
    width_part = moment1.shape[3]
    stored = jnp.sum(
        jnp.where(
            touched[:, :, None] == jnp.arange(number, dtype=jnp.int32)[None, None, :],
            slot_map[None, None, :],
            0,
        ),
        axis=2,
    )
    stored_all = stored.reshape(n_dp, n_own, TOUCH)
    group_rows = lax.dynamic_index_in_dim(stored_all, dp_at, 0, keepdims=False)
    flat_rows = group_rows.reshape(-1)
    my_list = lax.dynamic_index_in_dim(touched, dp_at * n_own + own_at, 0, keepdims=False)
    places = dispatch(row_insertion, my_list)
    stacked = (
        jnp.zeros((TOUCH * CAP, 2 * SITES), signals.dtype)
        .at[places]
        .set(jnp.concatenate([signals, cotangent], axis=1))
    )
    stacked = stacked.reshape(TOUCH, CAP, 2 * SITES)
    sig_slots = stacked[:, :, :SITES]
    cot_slots = stacked[:, :, SITES:]
    read_out = None
    outgoing = jnp.take(weights, flat_rows, axis=0).reshape(n_own, TOUCH, 2, piece_rows, WIDTH)
    arrived = lax.all_to_all(outgoing, "own", split_axis=0, concat_axis=3, tiled=True)
    read_in = arrived[0, :, 0]
    read_out = arrived[0, :, 1]
    preact = jnp.einsum("kcs,ksw->kcw", sig_slots, read_in, preferred_element_type=jnp.float32)
    gelu_val, slopes = gelu_parts(preact)
    hidden = gelu_val.astype(jnp.bfloat16)
    pred_slots = jnp.einsum(
        "kcw,ksw->kcs", hidden, read_out, preferred_element_type=jnp.float32
    ).astype(jnp.bfloat16)
    back_hidden = jnp.einsum(
        "kcs,ksw->kcw", cot_slots, read_out, preferred_element_type=jnp.float32
    )
    back_pre = (back_hidden * slopes).astype(jnp.bfloat16)
    grad_in = jnp.einsum("kcs,kcw->ksw", sig_slots, back_pre, preferred_element_type=jnp.float32)
    grad_out = jnp.einsum("kcs,kcw->ksw", cot_slots, hidden, preferred_element_type=jnp.float32)
    grads = jnp.stack([grad_in, grad_out], axis=1).astype(jnp.bfloat16)
    pieces = grads.reshape(TOUCH, 2, n_own, piece_rows, n_dp, width_part)
    pieces = pieces.transpose(4, 2, 0, 1, 3, 5).reshape(
        n_dp * n_own, TOUCH, 2, piece_rows, width_part
    )
    arrived_grad = lax.all_to_all(pieces, ("dp", "own"), split_axis=0, concat_axis=0, tiled=True)
    table = sum_by_insertion(stored.reshape(-1), arrived_grad, number).reshape(
        number, 2, piece_rows, width_part
    )
    own_params = lax.dynamic_slice_in_dim(weights, dp_at * width_part, width_part, 3).astype(
        jnp.float32
    )
    fresh_part, new_moment1, new_moment2 = adam_step(own_params, moment1, moment2, table)
    new_weights = lax.all_gather(fresh_part, "dp", axis=3, tiled=True)
    predicted = pred_slots.reshape(TOUCH * CAP, SITES)[places]
    return (predicted, new_weights, new_moment1, new_moment2)


def solution(mesh):
    in_specs = (
        P(("dp", "own"), None),
        P(("dp", "own"), None),
        P(("dp", "own")),
        P(),
        P(),
        P(None, None, "own", None),
        P(None, None, "own", "dp"),
        P(None, None, "own", "dp"),
    )
    out_specs = (
        P(("dp", "own"), None),
        P(None, None, "own", None),
        P(None, None, "own", "dp"),
        P(None, None, "own", "dp"),
    )
    return jax.shard_map(shards, mesh=mesh, in_specs=in_specs, out_specs=out_specs, check_vma=False)
```

```python
import functools
import math

import jax
import jax.numpy as jnp
from jax import lax
from jax.experimental import pallas as pl
from jax.experimental.pallas import tpu as pltpu
from jax.sharding import PartitionSpec as P

SITES = 384
WIDTH = 1024
TOUCH = 4
CAP = 128

MESH = pl.DeviceIdType.MESH

def _a2a_kernel(n_dp, n_own, full, x_ref, o_ref, send_sems, recv_sems, local_sem):
    dp_at = lax.axis_index("dp")
    own_at = lax.axis_index("own")
    if full:
        n = n_dp * n_own
        me = dp_at * n_own + own_at
        def dev(k):
            return (k // n_own, k % n_own)
    else:
        n = n_own
        me = own_at
        def dev(k):
            return (dp_at, k)
    barrier = pltpu.get_barrier_semaphore()

    def greet(i, c):
        peer = lax.rem(me + i, n)
        pl.semaphore_signal(barrier, 1, device_id=dev(peer), device_id_type=MESH)
        return c

    lax.fori_loop(1, n, greet, 0)
    pl.semaphore_wait(barrier, n - 1)
    local = pltpu.make_async_copy(x_ref.at[me], o_ref.at[me], local_sem)
    local.start()

    def send(i, c):
        peer = lax.rem(me + i, n)
        pltpu.make_async_remote_copy(
            src_ref=x_ref.at[peer], dst_ref=o_ref.at[me],
            send_sem=send_sems.at[peer], recv_sem=recv_sems.at[me],
            device_id=dev(peer), device_id_type=MESH,
        ).start()
        return c

    lax.fori_loop(1, n, send, 0)

    def finish(i, c):
        peer = lax.rem(me + i, n)
        src = lax.rem(me + n - i, n)
        pltpu.make_async_remote_copy(
            src_ref=x_ref.at[peer], dst_ref=o_ref.at[src],
            send_sem=send_sems.at[peer], recv_sem=recv_sems.at[src],
            device_id=dev(peer), device_id_type=MESH,
        ).wait_send()
        pltpu.make_async_remote_copy(
            src_ref=x_ref.at[peer], dst_ref=o_ref.at[src],
            send_sem=send_sems.at[peer], recv_sem=recv_sems.at[src],
            device_id=dev(src), device_id_type=MESH,
        ).wait_recv()
        return c

    lax.fori_loop(1, n, finish, 0)
    local.wait()


def exchange(x, n_dp, n_own, full, cid):
    n = x.shape[0]
    return pl.pallas_call(
        functools.partial(_a2a_kernel, n_dp, n_own, full),
        out_shape=jax.ShapeDtypeStruct(x.shape, x.dtype),
        in_specs=[pl.BlockSpec(memory_space=pl.ANY)],
        out_specs=pl.BlockSpec(memory_space=pl.ANY),
        scratch_shapes=[
            pltpu.SemaphoreType.DMA((n,)),
            pltpu.SemaphoreType.DMA((n,)),
            pltpu.SemaphoreType.DMA,
        ],
        compiler_params=pltpu.CompilerParams(collective_id=cid, has_side_effects=True),
    )(x)


gelu_coef = math.sqrt(2.0 / math.pi)
cubic_coef = 0.044715
learn_rate = 0.01
highest = lax.Precision.HIGHEST


def gelu_parts(preact):
    tanh_input = gelu_coef * (preact + cubic_coef * preact * preact * preact)
    tangent = jnp.tanh(tanh_input)
    gelu_val = 0.5 * preact * (1.0 + tangent)
    slopes = 0.5 * (1.0 + tangent) + 0.5 * preact * (1.0 - tangent * tangent) * gelu_coef * (
        1.0 + 3.0 * cubic_coef * preact * preact
    )
    return (gelu_val, slopes)


def dispatch(row_ids, listed):
    match_table = (row_ids[:, None] == listed[None, :]).astype(jnp.int32)
    running = jnp.cumsum(match_table, axis=0) - 1
    slot_of = jnp.sum(match_table * jnp.arange(listed.shape[0], dtype=jnp.int32)[None, :], axis=1)
    within = jnp.sum(match_table * running, axis=1)
    return slot_of * CAP + within


def adam_step(params, moment_one, moment_two, gradient):
    moment_one = 0.9 * moment_one + 0.1 * gradient
    moment_two = 0.999 * moment_two + 0.001 * gradient * gradient
    correct_one = 1.0 - 0.9**10
    correct_two = 1.0 - 0.999**10
    updated = params - learn_rate * (moment_one / correct_one) / (
        jnp.sqrt(moment_two / correct_two) + 1e-08
    )
    return (updated.astype(jnp.bfloat16), moment_one, moment_two)


def sum_by_insertion(item_rows, arrived_grad, number):
    one_hot = (jnp.arange(number, dtype=jnp.int32)[:, None] == item_rows[None, :]).astype(
        arrived_grad.dtype
    )
    flat_grad = arrived_grad.reshape(item_rows.shape[0], -1)
    return jnp.dot(one_hot, flat_grad, preferred_element_type=jnp.float32)


def shards(signals, cotangent, row_insertion, touched, slot_map, weights, moment1, moment2):
    n_own = lax.axis_size("own")
    n_dp = lax.axis_size("dp")
    dp_at = lax.axis_index("dp")
    own_at = lax.axis_index("own")
    number = weights.shape[0]
    piece_rows = weights.shape[2]
    width_part = moment1.shape[3]
    stored = jnp.sum(
        jnp.where(
            touched[:, :, None] == jnp.arange(number, dtype=jnp.int32)[None, None, :],
            slot_map[None, None, :],
            0,
        ),
        axis=2,
    )
    stored_all = stored.reshape(n_dp, n_own, TOUCH)
    group_rows = lax.dynamic_index_in_dim(stored_all, dp_at, 0, keepdims=False)
    flat_rows = group_rows.reshape(-1)
    my_list = lax.dynamic_index_in_dim(touched, dp_at * n_own + own_at, 0, keepdims=False)
    places = dispatch(row_insertion, my_list)
    stacked = (
        jnp.zeros((TOUCH * CAP, 2 * SITES), signals.dtype)
        .at[places]
        .set(jnp.concatenate([signals, cotangent], axis=1))
    )
    stacked = stacked.reshape(TOUCH, CAP, 2 * SITES)
    sig_slots = stacked[:, :, :SITES]
    cot_slots = stacked[:, :, SITES:]
    read_out = None
    outgoing = jnp.take(weights, flat_rows, axis=0).reshape(n_own, TOUCH, 2, piece_rows, WIDTH)
    arrived = lax.all_to_all(outgoing, "own", split_axis=0, concat_axis=3, tiled=True)
    read_in = arrived[0, :, 0]
    read_out = arrived[0, :, 1]
    preact = jnp.einsum("kcs,ksw->kcw", sig_slots, read_in, preferred_element_type=jnp.float32)
    gelu_val, slopes = gelu_parts(preact)
    hidden = gelu_val.astype(jnp.bfloat16)
    pred_slots = jnp.einsum(
        "kcw,ksw->kcs", hidden, read_out, preferred_element_type=jnp.float32
    ).astype(jnp.bfloat16)
    back_hidden = jnp.einsum(
        "kcs,ksw->kcw", cot_slots, read_out, preferred_element_type=jnp.float32
    )
    back_pre = (back_hidden * slopes).astype(jnp.bfloat16)
    grad_in = jnp.einsum("kcs,kcw->ksw", sig_slots, back_pre, preferred_element_type=jnp.float32)
    grad_out = jnp.einsum("kcs,kcw->ksw", cot_slots, hidden, preferred_element_type=jnp.float32)
    grads = jnp.stack([grad_in, grad_out], axis=1).astype(jnp.bfloat16)
    pieces = grads.reshape(TOUCH, 2, n_own, piece_rows, n_dp, width_part)
    pieces = pieces.transpose(4, 2, 0, 1, 3, 5).reshape(
        n_dp * n_own, TOUCH, 2, piece_rows, width_part
    )
    arrived_grad = exchange(
        pieces.reshape(n_dp * n_own, TOUCH * 2 * piece_rows, width_part), n_dp, n_own, True, 0
    )
    table = sum_by_insertion(stored.reshape(-1), arrived_grad, number).reshape(
        number, 2, piece_rows, width_part
    )
    own_params = lax.dynamic_slice_in_dim(weights, dp_at * width_part, width_part, 3).astype(
        jnp.float32
    )
    fresh_part, new_moment1, new_moment2 = adam_step(own_params, moment1, moment2, table)
    new_weights = lax.all_gather(fresh_part, "dp", axis=3, tiled=True)
    predicted = pred_slots.reshape(TOUCH * CAP, SITES)[places]
    return (predicted, new_weights, new_moment1, new_moment2)


def solution(mesh):
    in_specs = (
        P(("dp", "own"), None),
        P(("dp", "own"), None),
        P(("dp", "own")),
        P(),
        P(),
        P(None, None, "own", None),
        P(None, None, "own", "dp"),
        P(None, None, "own", "dp"),
    )
    out_specs = (
        P(("dp", "own"), None),
        P(None, None, "own", None),
        P(None, None, "own", "dp"),
        P(None, None, "own", "dp"),
    )
    return jax.shard_map(shards, mesh=mesh, in_specs=in_specs, out_specs=out_specs, check_vma=False)
```

```python
import functools
import math

import jax
import jax.numpy as jnp
from jax import lax
from jax.experimental import pallas as pl
from jax.experimental.pallas import tpu as pltpu
from jax.sharding import PartitionSpec as P

SITES = 384
WIDTH = 1024
TOUCH = 4
CAP = 128

MESH = pl.DeviceIdType.MESH

def _a2a_kernel(n_dp, n_own, full, x_ref, o_ref, send_sems, recv_sems, local_sem):
    dp_at = lax.axis_index("dp")
    own_at = lax.axis_index("own")
    if full:
        n = n_dp * n_own
        me = dp_at * n_own + own_at
        def dev(k):
            return (k // n_own, k % n_own)
    else:
        n = n_own
        me = own_at
        def dev(k):
            return (dp_at, k)
    barrier = pltpu.get_barrier_semaphore()

    def greet(i, c):
        peer = lax.rem(me + i, n)
        pl.semaphore_signal(barrier, 1, device_id=dev(peer), device_id_type=MESH)
        return c

    lax.fori_loop(1, n, greet, 0)
    pl.semaphore_wait(barrier, n - 1)
    local = pltpu.make_async_copy(x_ref.at[me], o_ref.at[me], local_sem)
    local.start()

    def send(i, c):
        peer = lax.rem(me + i, n)
        pltpu.make_async_remote_copy(
            src_ref=x_ref.at[peer], dst_ref=o_ref.at[me],
            send_sem=send_sems.at[peer], recv_sem=recv_sems.at[me],
            device_id=dev(peer), device_id_type=MESH,
        ).start()
        return c

    lax.fori_loop(1, n, send, 0)

    def finish(i, c):
        peer = lax.rem(me + i, n)
        src = lax.rem(me + n - i, n)
        pltpu.make_async_remote_copy(
            src_ref=x_ref.at[peer], dst_ref=o_ref.at[src],
            send_sem=send_sems.at[peer], recv_sem=recv_sems.at[src],
            device_id=dev(peer), device_id_type=MESH,
        ).wait_send()
        pltpu.make_async_remote_copy(
            src_ref=x_ref.at[peer], dst_ref=o_ref.at[src],
            send_sem=send_sems.at[peer], recv_sem=recv_sems.at[src],
            device_id=dev(src), device_id_type=MESH,
        ).wait_recv()
        return c

    lax.fori_loop(1, n, finish, 0)
    local.wait()


def exchange(x, n_dp, n_own, full, cid):
    n = x.shape[0]
    return pl.pallas_call(
        functools.partial(_a2a_kernel, n_dp, n_own, full),
        out_shape=jax.ShapeDtypeStruct(x.shape, x.dtype),
        in_specs=[pl.BlockSpec(memory_space=pl.ANY)],
        out_specs=pl.BlockSpec(memory_space=pl.ANY),
        scratch_shapes=[
            pltpu.SemaphoreType.DMA((n,)),
            pltpu.SemaphoreType.DMA((n,)),
            pltpu.SemaphoreType.DMA,
        ],
        compiler_params=pltpu.CompilerParams(collective_id=cid, has_side_effects=True),
    )(x)


gelu_coef = math.sqrt(2.0 / math.pi)
cubic_coef = 0.044715
learn_rate = 0.01
highest = lax.Precision.HIGHEST


def gelu_parts(preact):
    tanh_input = gelu_coef * (preact + cubic_coef * preact * preact * preact)
    tangent = jnp.tanh(tanh_input)
    gelu_val = 0.5 * preact * (1.0 + tangent)
    slopes = 0.5 * (1.0 + tangent) + 0.5 * preact * (1.0 - tangent * tangent) * gelu_coef * (
        1.0 + 3.0 * cubic_coef * preact * preact
    )
    return (gelu_val, slopes)


def dispatch(row_ids, listed):
    match_table = (row_ids[:, None] == listed[None, :]).astype(jnp.int32)
    running = jnp.cumsum(match_table, axis=0) - 1
    slot_of = jnp.sum(match_table * jnp.arange(listed.shape[0], dtype=jnp.int32)[None, :], axis=1)
    within = jnp.sum(match_table * running, axis=1)
    return slot_of * CAP + within


def adam_step(params, moment_one, moment_two, gradient):
    moment_one = 0.9 * moment_one + 0.1 * gradient
    moment_two = 0.999 * moment_two + 0.001 * gradient * gradient
    correct_one = 1.0 - 0.9**10
    correct_two = 1.0 - 0.999**10
    updated = params - learn_rate * (moment_one / correct_one) / (
        jnp.sqrt(moment_two / correct_two) + 1e-08
    )
    return (updated.astype(jnp.bfloat16), moment_one, moment_two)


def sum_by_insertion(item_rows, arrived_grad, number):
    one_hot = (jnp.arange(number, dtype=jnp.int32)[:, None] == item_rows[None, :]).astype(
        arrived_grad.dtype
    )
    flat_grad = arrived_grad.reshape(item_rows.shape[0], -1)
    return jnp.dot(one_hot, flat_grad, preferred_element_type=jnp.float32)


def shards(signals, cotangent, row_insertion, touched, slot_map, weights, moment1, moment2):
    n_own = lax.axis_size("own")
    n_dp = lax.axis_size("dp")
    dp_at = lax.axis_index("dp")
    own_at = lax.axis_index("own")
    number = weights.shape[0]
    piece_rows = weights.shape[2]
    width_part = moment1.shape[3]
    pairs = n_dp * TOUCH
    stored = jnp.sum(
        jnp.where(
            touched[:, :, None] == jnp.arange(number, dtype=jnp.int32)[None, None, :],
            slot_map[None, None, :],
            0,
        ),
        axis=2,
    )
    peer_rows = stored.reshape(n_dp, n_own, TOUCH).transpose(1, 0, 2).reshape(-1)
    my_list = lax.dynamic_index_in_dim(touched, dp_at * n_own + own_at, 0, keepdims=False)
    places = dispatch(row_insertion, my_list)
    stacked = (
        jnp.zeros((TOUCH * CAP, 2 * SITES), signals.dtype)
        .at[places]
        .set(jnp.concatenate([signals, cotangent], axis=1))
    )
    stacked = lax.all_gather(stacked.reshape(TOUCH, CAP, 2 * SITES), "dp", axis=0, tiled=True)
    stacked = stacked.reshape(pairs, CAP, 2 * SITES)
    sig_slots = stacked[:, :, :SITES]
    cot_slots = stacked[:, :, SITES:]
    my_width = lax.dynamic_slice_in_dim(weights, dp_at * width_part, width_part, 3)
    outgoing = jnp.take(my_width, peer_rows, axis=0).reshape(
        n_own, pairs, 2, piece_rows, width_part
    )
    arrived = lax.all_to_all(outgoing, "own", split_axis=0, concat_axis=0, tiled=True)
    arrived = arrived.transpose(1, 2, 0, 3, 4).reshape(pairs, 2, SITES, width_part)
    read_in = arrived[:, 0]
    read_out = arrived[:, 1]
    preact = jnp.einsum("kcs,ksw->kcw", sig_slots, read_in, preferred_element_type=jnp.float32)
    gelu_val, slopes = gelu_parts(preact)
    hidden = gelu_val.astype(jnp.bfloat16)
    pred_part = jnp.einsum("kcw,ksw->kcs", hidden, read_out, preferred_element_type=jnp.float32)
    back_hidden = jnp.einsum(
        "kcs,ksw->kcw", cot_slots, read_out, preferred_element_type=jnp.float32
    )
    back_pre = (back_hidden * slopes).astype(jnp.bfloat16)
    grad_in = jnp.einsum("kcs,kcw->ksw", sig_slots, back_pre, preferred_element_type=jnp.float32)
    grad_out = jnp.einsum("kcs,kcw->ksw", cot_slots, hidden, preferred_element_type=jnp.float32)
    pred_slots = lax.psum_scatter(pred_part, "dp", scatter_dimension=0, tiled=True)
    pred_slots = pred_slots.astype(jnp.bfloat16)
    grads = jnp.stack([grad_in, grad_out], axis=1).astype(jnp.bfloat16)
    pieces = grads.reshape(pairs, 2, n_own, piece_rows, width_part).transpose(2, 0, 1, 3, 4)
    arrived_grad = lax.all_to_all(pieces, "own", split_axis=0, concat_axis=0, tiled=True)
    table = sum_by_insertion(peer_rows, arrived_grad, number).reshape(
        number, 2, piece_rows, width_part
    )
    own_params = my_width.astype(jnp.float32)
    fresh_part, new_moment1, new_moment2 = adam_step(own_params, moment1, moment2, table)
    new_weights = lax.all_gather(fresh_part, "dp", axis=3, tiled=True)
    predicted = pred_slots.reshape(TOUCH * CAP, SITES)[places]
    return (predicted, new_weights, new_moment1, new_moment2)


def solution(mesh):
    in_specs = (
        P(("dp", "own"), None),
        P(("dp", "own"), None),
        P(("dp", "own")),
        P(),
        P(),
        P(None, None, "own", None),
        P(None, None, "own", "dp"),
        P(None, None, "own", "dp"),
    )
    out_specs = (
        P(("dp", "own"), None),
        P(None, None, "own", None),
        P(None, None, "own", "dp"),
        P(None, None, "own", "dp"),
    )
    return jax.shard_map(shards, mesh=mesh, in_specs=in_specs, out_specs=out_specs, check_vma=False)
```

```python
import functools
import math

import jax
import jax.numpy as jnp
from jax import lax
from jax.experimental import pallas as pl
from jax.experimental.pallas import tpu as pltpu
from jax.sharding import PartitionSpec as P

SITES = 384
WIDTH = 1024
TOUCH = 4
CAP = 128

MESH = pl.DeviceIdType.MESH

def _a2a_kernel(n_dp, n_own, full, x_ref, o_ref, send_sems, recv_sems, local_sem):
    dp_at = lax.axis_index("dp")
    own_at = lax.axis_index("own")
    if full:
        n = n_dp * n_own
        me = dp_at * n_own + own_at
        def dev(k):
            return (k // n_own, k % n_own)
    else:
        n = n_own
        me = own_at
        def dev(k):
            return (dp_at, k)
    barrier = pltpu.get_barrier_semaphore()

    def greet(i, c):
        peer = lax.rem(me + i, n)
        pl.semaphore_signal(barrier, 1, device_id=dev(peer), device_id_type=MESH)
        return c

    lax.fori_loop(1, n, greet, 0)
    pl.semaphore_wait(barrier, n - 1)
    local = pltpu.make_async_copy(x_ref.at[me], o_ref.at[me], local_sem)
    local.start()

    def send(i, c):
        peer = lax.rem(me + i, n)
        pltpu.make_async_remote_copy(
            src_ref=x_ref.at[peer], dst_ref=o_ref.at[me],
            send_sem=send_sems.at[peer], recv_sem=recv_sems.at[me],
            device_id=dev(peer), device_id_type=MESH,
        ).start()
        return c

    lax.fori_loop(1, n, send, 0)

    def finish(i, c):
        peer = lax.rem(me + i, n)
        src = lax.rem(me + n - i, n)
        pltpu.make_async_remote_copy(
            src_ref=x_ref.at[peer], dst_ref=o_ref.at[src],
            send_sem=send_sems.at[peer], recv_sem=recv_sems.at[src],
            device_id=dev(peer), device_id_type=MESH,
        ).wait_send()
        pltpu.make_async_remote_copy(
            src_ref=x_ref.at[peer], dst_ref=o_ref.at[src],
            send_sem=send_sems.at[peer], recv_sem=recv_sems.at[src],
            device_id=dev(src), device_id_type=MESH,
        ).wait_recv()
        return c

    lax.fori_loop(1, n, finish, 0)
    local.wait()


def exchange(x, n_dp, n_own, full, cid):
    n = x.shape[0]
    return pl.pallas_call(
        functools.partial(_a2a_kernel, n_dp, n_own, full),
        out_shape=jax.ShapeDtypeStruct(x.shape, x.dtype),
        in_specs=[pl.BlockSpec(memory_space=pl.ANY)],
        out_specs=pl.BlockSpec(memory_space=pl.ANY),
        scratch_shapes=[
            pltpu.SemaphoreType.DMA((n,)),
            pltpu.SemaphoreType.DMA((n,)),
            pltpu.SemaphoreType.DMA,
        ],
        compiler_params=pltpu.CompilerParams(collective_id=cid, has_side_effects=True),
    )(x)


gelu_coef = math.sqrt(2.0 / math.pi)
cubic_coef = 0.044715
learn_rate = 0.01
highest = lax.Precision.HIGHEST


def gelu_parts(preact):
    tanh_input = gelu_coef * (preact + cubic_coef * preact * preact * preact)
    tangent = jnp.tanh(tanh_input)
    gelu_val = 0.5 * preact * (1.0 + tangent)
    slopes = 0.5 * (1.0 + tangent) + 0.5 * preact * (1.0 - tangent * tangent) * gelu_coef * (
        1.0 + 3.0 * cubic_coef * preact * preact
    )
    return (gelu_val, slopes)


def dispatch(row_ids, listed):
    match_table = (row_ids[:, None] == listed[None, :]).astype(jnp.int32)
    running = jnp.cumsum(match_table, axis=0) - 1
    slot_of = jnp.sum(match_table * jnp.arange(listed.shape[0], dtype=jnp.int32)[None, :], axis=1)
    within = jnp.sum(match_table * running, axis=1)
    return slot_of * CAP + within


def adam_step(params, moment_one, moment_two, gradient):
    moment_one = 0.9 * moment_one + 0.1 * gradient
    moment_two = 0.999 * moment_two + 0.001 * gradient * gradient
    correct_one = 1.0 - 0.9**10
    correct_two = 1.0 - 0.999**10
    updated = params - learn_rate * (moment_one / correct_one) / (
        jnp.sqrt(moment_two / correct_two) + 1e-08
    )
    return (updated.astype(jnp.bfloat16), moment_one, moment_two)


def sum_by_insertion(item_rows, arrived_grad, number):
    one_hot = (jnp.arange(number, dtype=jnp.int32)[:, None] == item_rows[None, :]).astype(
        arrived_grad.dtype
    )
    flat_grad = arrived_grad.reshape(item_rows.shape[0], -1)
    return jnp.dot(one_hot, flat_grad, preferred_element_type=jnp.float32)


def shards(signals, cotangent, row_insertion, touched, slot_map, weights, moment1, moment2):
    n_own = lax.axis_size("own")
    n_dp = lax.axis_size("dp")
    dp_at = lax.axis_index("dp")
    own_at = lax.axis_index("own")
    number = weights.shape[0]
    piece_rows = weights.shape[2]
    width_part = moment1.shape[3]
    pairs = n_dp * TOUCH
    stored = jnp.sum(
        jnp.where(
            touched[:, :, None] == jnp.arange(number, dtype=jnp.int32)[None, None, :],
            slot_map[None, None, :],
            0,
        ),
        axis=2,
    )
    peer_rows = stored.reshape(n_dp, n_own, TOUCH).transpose(1, 0, 2).reshape(-1)
    my_list = lax.dynamic_index_in_dim(touched, dp_at * n_own + own_at, 0, keepdims=False)
    places = dispatch(row_insertion, my_list)
    stacked = (
        jnp.zeros((TOUCH * CAP, 2 * SITES), signals.dtype)
        .at[places]
        .set(jnp.concatenate([signals, cotangent], axis=1))
    )
    stacked = lax.all_gather(stacked.reshape(TOUCH, CAP, 2 * SITES), "dp", axis=0, tiled=True)
    stacked = stacked.reshape(pairs, CAP, 2 * SITES)
    sig_slots = stacked[:, :, :SITES]
    cot_slots = stacked[:, :, SITES:]
    my_width = lax.dynamic_slice_in_dim(weights, dp_at * width_part, width_part, 3)
    outgoing = jnp.take(my_width, peer_rows, axis=0).reshape(
        n_own, pairs, 2, piece_rows, width_part
    )
    arrived = lax.all_to_all(outgoing, "own", split_axis=0, concat_axis=0, tiled=True)
    arrived = arrived.transpose(1, 2, 0, 3, 4).reshape(pairs, 2, SITES, width_part)
    read_in = arrived[:, 0]
    read_out = arrived[:, 1]
    preact = jnp.einsum("kcs,ksw->kcw", sig_slots, read_in, preferred_element_type=jnp.float32)
    gelu_val, slopes = gelu_parts(preact)
    hidden = gelu_val.astype(jnp.bfloat16)
    pred_part = jnp.einsum("kcw,ksw->kcs", hidden, read_out, preferred_element_type=jnp.float32)
    back_hidden = jnp.einsum(
        "kcs,ksw->kcw", cot_slots, read_out, preferred_element_type=jnp.float32
    )
    back_pre = (back_hidden * slopes).astype(jnp.bfloat16)
    grad_in = jnp.einsum("kcs,kcw->ksw", sig_slots, back_pre, preferred_element_type=jnp.float32)
    grad_out = jnp.einsum("kcs,kcw->ksw", cot_slots, hidden, preferred_element_type=jnp.float32)
    grads = jnp.stack([grad_in, grad_out], axis=1).astype(jnp.bfloat16)
    pred_part, grads = lax.optimization_barrier((pred_part, grads))
    pred_slots = lax.psum_scatter(pred_part, "dp", scatter_dimension=0, tiled=True)
    pieces = grads.reshape(pairs, 2, n_own, piece_rows, width_part).transpose(2, 0, 1, 3, 4)
    arrived_grad = lax.all_to_all(pieces, "own", split_axis=0, concat_axis=0, tiled=True)
    arrived_grad, pred_slots = lax.optimization_barrier((arrived_grad, pred_slots))
    pred_slots = pred_slots.astype(jnp.bfloat16)
    table = sum_by_insertion(peer_rows, arrived_grad, number).reshape(
        number, 2, piece_rows, width_part
    )
    own_params = my_width.astype(jnp.float32)
    fresh_part, new_moment1, new_moment2 = adam_step(own_params, moment1, moment2, table)
    new_weights = lax.all_gather(fresh_part, "dp", axis=3, tiled=True)
    predicted = pred_slots.reshape(TOUCH * CAP, SITES)[places]
    return (predicted, new_weights, new_moment1, new_moment2)


def solution(mesh):
    in_specs = (
        P(("dp", "own"), None),
        P(("dp", "own"), None),
        P(("dp", "own")),
        P(),
        P(),
        P(None, None, "own", None),
        P(None, None, "own", "dp"),
        P(None, None, "own", "dp"),
    )
    out_specs = (
        P(("dp", "own"), None),
        P(None, None, "own", None),
        P(None, None, "own", "dp"),
        P(None, None, "own", "dp"),
    )
    return jax.shard_map(shards, mesh=mesh, in_specs=in_specs, out_specs=out_specs, check_vma=False)
```

```python
import functools
import math

import jax
import jax.numpy as jnp
from jax import lax
from jax.experimental import pallas as pl
from jax.experimental.pallas import tpu as pltpu
from jax.sharding import PartitionSpec as P

SITES = 384
WIDTH = 1024
TOUCH = 4
CAP = 128

MESH = pl.DeviceIdType.MESH

def _a2a_kernel(n_dp, n_own, full, x_ref, o_ref, send_sems, recv_sems, local_sem):
    dp_at = lax.axis_index("dp")
    own_at = lax.axis_index("own")
    if full:
        n = n_dp * n_own
        me = dp_at * n_own + own_at
        def dev(k):
            return (k // n_own, k % n_own)
    else:
        n = n_own
        me = own_at
        def dev(k):
            return (dp_at, k)
    barrier = pltpu.get_barrier_semaphore()

    def greet(i, c):
        peer = lax.rem(me + i, n)
        pl.semaphore_signal(barrier, 1, device_id=dev(peer), device_id_type=MESH)
        return c

    lax.fori_loop(1, n, greet, 0)
    pl.semaphore_wait(barrier, n - 1)
    local = pltpu.make_async_copy(x_ref.at[me], o_ref.at[me], local_sem)
    local.start()

    def send(i, c):
        peer = lax.rem(me + i, n)
        pltpu.make_async_remote_copy(
            src_ref=x_ref.at[peer], dst_ref=o_ref.at[me],
            send_sem=send_sems.at[peer], recv_sem=recv_sems.at[me],
            device_id=dev(peer), device_id_type=MESH,
        ).start()
        return c

    lax.fori_loop(1, n, send, 0)

    def finish(i, c):
        peer = lax.rem(me + i, n)
        src = lax.rem(me + n - i, n)
        pltpu.make_async_remote_copy(
            src_ref=x_ref.at[peer], dst_ref=o_ref.at[src],
            send_sem=send_sems.at[peer], recv_sem=recv_sems.at[src],
            device_id=dev(peer), device_id_type=MESH,
        ).wait_send()
        pltpu.make_async_remote_copy(
            src_ref=x_ref.at[peer], dst_ref=o_ref.at[src],
            send_sem=send_sems.at[peer], recv_sem=recv_sems.at[src],
            device_id=dev(src), device_id_type=MESH,
        ).wait_recv()
        return c

    lax.fori_loop(1, n, finish, 0)
    local.wait()


def exchange(x, n_dp, n_own, full, cid):
    n = x.shape[0]
    return pl.pallas_call(
        functools.partial(_a2a_kernel, n_dp, n_own, full),
        out_shape=jax.ShapeDtypeStruct(x.shape, x.dtype),
        in_specs=[pl.BlockSpec(memory_space=pl.ANY)],
        out_specs=pl.BlockSpec(memory_space=pl.ANY),
        scratch_shapes=[
            pltpu.SemaphoreType.DMA((n,)),
            pltpu.SemaphoreType.DMA((n,)),
            pltpu.SemaphoreType.DMA,
        ],
        compiler_params=pltpu.CompilerParams(collective_id=cid, has_side_effects=True),
    )(x)


gelu_coef = math.sqrt(2.0 / math.pi)
cubic_coef = 0.044715
learn_rate = 0.01
highest = lax.Precision.HIGHEST


def gelu_parts(preact):
    tanh_input = gelu_coef * (preact + cubic_coef * preact * preact * preact)
    tangent = jnp.tanh(tanh_input)
    gelu_val = 0.5 * preact * (1.0 + tangent)
    slopes = 0.5 * (1.0 + tangent) + 0.5 * preact * (1.0 - tangent * tangent) * gelu_coef * (
        1.0 + 3.0 * cubic_coef * preact * preact
    )
    return (gelu_val, slopes)


def dispatch(row_ids, listed):
    match_table = (row_ids[:, None] == listed[None, :]).astype(jnp.int32)
    running = jnp.cumsum(match_table, axis=0) - 1
    slot_of = jnp.sum(match_table * jnp.arange(listed.shape[0], dtype=jnp.int32)[None, :], axis=1)
    within = jnp.sum(match_table * running, axis=1)
    return slot_of * CAP + within


def adam_step(params, moment_one, moment_two, gradient):
    moment_one = 0.9 * moment_one + 0.1 * gradient
    moment_two = 0.999 * moment_two + 0.001 * gradient * gradient
    correct_one = 1.0 - 0.9**10
    correct_two = 1.0 - 0.999**10
    updated = params - learn_rate * (moment_one / correct_one) / (
        jnp.sqrt(moment_two / correct_two) + 1e-08
    )
    return (updated.astype(jnp.bfloat16), moment_one, moment_two)


def sum_by_insertion(item_rows, arrived_grad, number):
    one_hot = (jnp.arange(number, dtype=jnp.int32)[:, None] == item_rows[None, :]).astype(
        arrived_grad.dtype
    )
    flat_grad = arrived_grad.reshape(item_rows.shape[0], -1)
    return jnp.dot(one_hot, flat_grad, preferred_element_type=jnp.float32)


def shards(signals, cotangent, row_insertion, touched, slot_map, weights, moment1, moment2):
    n_own = lax.axis_size("own")
    n_dp = lax.axis_size("dp")
    dp_at = lax.axis_index("dp")
    own_at = lax.axis_index("own")
    number = weights.shape[0]
    piece_rows = weights.shape[2]
    width_part = moment1.shape[3]
    pairs = n_dp * TOUCH
    stored = jnp.sum(
        jnp.where(
            touched[:, :, None] == jnp.arange(number, dtype=jnp.int32)[None, None, :],
            slot_map[None, None, :],
            0,
        ),
        axis=2,
    )
    peer_rows = stored.reshape(n_dp, n_own, TOUCH).transpose(1, 0, 2).reshape(-1)
    my_list = lax.dynamic_index_in_dim(touched, dp_at * n_own + own_at, 0, keepdims=False)
    places = dispatch(row_insertion, my_list)
    stacked = (
        jnp.zeros((TOUCH * CAP, 2 * SITES), signals.dtype)
        .at[places]
        .set(jnp.concatenate([signals, cotangent], axis=1))
    )
    stacked = lax.all_gather(stacked.reshape(TOUCH, CAP, 2 * SITES), "dp", axis=0, tiled=True)
    stacked = stacked.reshape(pairs, CAP, 2 * SITES)
    sig_slots = stacked[:, :, :SITES]
    cot_slots = stacked[:, :, SITES:]
    my_width = lax.dynamic_slice_in_dim(weights, dp_at * width_part, width_part, 3)
    pick = (peer_rows[:, None] == jnp.arange(number, dtype=jnp.int32)[None, :]).astype(weights.dtype)
    outgoing = jnp.dot(
        pick, my_width.reshape(number, -1), preferred_element_type=jnp.float32
    ).astype(weights.dtype)
    outgoing = outgoing.reshape(n_own, pairs, 2, piece_rows, width_part)
    arrived = lax.all_to_all(outgoing, "own", split_axis=0, concat_axis=0, tiled=True)
    arrived = arrived.transpose(1, 2, 0, 3, 4).reshape(pairs, 2, SITES, width_part)
    read_in = arrived[:, 0]
    read_out = arrived[:, 1]
    preact = jnp.einsum("kcs,ksw->kcw", sig_slots, read_in, preferred_element_type=jnp.float32)
    gelu_val, slopes = gelu_parts(preact)
    hidden = gelu_val.astype(jnp.bfloat16)
    pred_part = jnp.einsum("kcw,ksw->kcs", hidden, read_out, preferred_element_type=jnp.float32)
    back_hidden = jnp.einsum(
        "kcs,ksw->kcw", cot_slots, read_out, preferred_element_type=jnp.float32
    )
    back_pre = (back_hidden * slopes).astype(jnp.bfloat16)
    grad_in = jnp.einsum("kcs,kcw->ksw", sig_slots, back_pre, preferred_element_type=jnp.float32)
    grad_out = jnp.einsum("kcs,kcw->ksw", cot_slots, hidden, preferred_element_type=jnp.float32)
    grads = jnp.stack([grad_in, grad_out], axis=1).astype(jnp.bfloat16)
    pred_part, grads = lax.optimization_barrier((pred_part, grads))
    pred_slots = lax.psum_scatter(pred_part, "dp", scatter_dimension=0, tiled=True)
    pieces = grads.reshape(pairs, 2, n_own, piece_rows, width_part).transpose(2, 0, 1, 3, 4)
    arrived_grad = lax.all_to_all(pieces, "own", split_axis=0, concat_axis=0, tiled=True)
    arrived_grad, pred_slots = lax.optimization_barrier((arrived_grad, pred_slots))
    pred_slots = pred_slots.astype(jnp.bfloat16)
    table = sum_by_insertion(peer_rows, arrived_grad, number).reshape(
        number, 2, piece_rows, width_part
    )
    own_params = my_width.astype(jnp.float32)
    fresh_part, new_moment1, new_moment2 = adam_step(own_params, moment1, moment2, table)
    new_weights = lax.all_gather(fresh_part, "dp", axis=0, tiled=False)
    new_weights = new_weights.transpose(1, 2, 3, 0, 4).reshape(weights.shape)
    predicted = pred_slots.reshape(TOUCH * CAP, SITES)[places]
    return (predicted, new_weights, new_moment1, new_moment2)


def solution(mesh):
    in_specs = (
        P(("dp", "own"), None),
        P(("dp", "own"), None),
        P(("dp", "own")),
        P(),
        P(),
        P(None, None, "own", None),
        P(None, None, "own", "dp"),
        P(None, None, "own", "dp"),
    )
    out_specs = (
        P(("dp", "own"), None),
        P(None, None, "own", None),
        P(None, None, "own", "dp"),
        P(None, None, "own", "dp"),
    )
    return jax.shard_map(shards, mesh=mesh, in_specs=in_specs, out_specs=out_specs, check_vma=False)
```

```python
import functools
import math

import jax
import jax.numpy as jnp
from jax import lax
from jax.experimental import pallas as pl
from jax.experimental.pallas import tpu as pltpu
from jax.sharding import PartitionSpec as P

SITES = 384
WIDTH = 1024
TOUCH = 4
CAP = 128

MESH = pl.DeviceIdType.MESH

def _a2a_kernel(n_dp, n_own, full, x_ref, o_ref, send_sems, recv_sems, local_sem):
    dp_at = lax.axis_index("dp")
    own_at = lax.axis_index("own")
    if full:
        n = n_dp * n_own
        me = dp_at * n_own + own_at
        def dev(k):
            return (k // n_own, k % n_own)
    else:
        n = n_own
        me = own_at
        def dev(k):
            return (dp_at, k)
    barrier = pltpu.get_barrier_semaphore()

    def greet(i, c):
        peer = lax.rem(me + i, n)
        pl.semaphore_signal(barrier, 1, device_id=dev(peer), device_id_type=MESH)
        return c

    lax.fori_loop(1, n, greet, 0)
    pl.semaphore_wait(barrier, n - 1)
    local = pltpu.make_async_copy(x_ref.at[me], o_ref.at[me], local_sem)
    local.start()

    def send(i, c):
        peer = lax.rem(me + i, n)
        pltpu.make_async_remote_copy(
            src_ref=x_ref.at[peer], dst_ref=o_ref.at[me],
            send_sem=send_sems.at[peer], recv_sem=recv_sems.at[me],
            device_id=dev(peer), device_id_type=MESH,
        ).start()
        return c

    lax.fori_loop(1, n, send, 0)

    def finish(i, c):
        peer = lax.rem(me + i, n)
        src = lax.rem(me + n - i, n)
        pltpu.make_async_remote_copy(
            src_ref=x_ref.at[peer], dst_ref=o_ref.at[src],
            send_sem=send_sems.at[peer], recv_sem=recv_sems.at[src],
            device_id=dev(peer), device_id_type=MESH,
        ).wait_send()
        pltpu.make_async_remote_copy(
            src_ref=x_ref.at[peer], dst_ref=o_ref.at[src],
            send_sem=send_sems.at[peer], recv_sem=recv_sems.at[src],
            device_id=dev(src), device_id_type=MESH,
        ).wait_recv()
        return c

    lax.fori_loop(1, n, finish, 0)
    local.wait()


def exchange(x, n_dp, n_own, full, cid):
    n = x.shape[0]
    return pl.pallas_call(
        functools.partial(_a2a_kernel, n_dp, n_own, full),
        out_shape=jax.ShapeDtypeStruct(x.shape, x.dtype),
        in_specs=[pl.BlockSpec(memory_space=pl.ANY)],
        out_specs=pl.BlockSpec(memory_space=pl.ANY),
        scratch_shapes=[
            pltpu.SemaphoreType.DMA((n,)),
            pltpu.SemaphoreType.DMA((n,)),
            pltpu.SemaphoreType.DMA,
        ],
        compiler_params=pltpu.CompilerParams(collective_id=cid, has_side_effects=True),
    )(x)


gelu_coef = math.sqrt(2.0 / math.pi)
cubic_coef = 0.044715
learn_rate = 0.01
highest = lax.Precision.HIGHEST


def gelu_parts(preact):
    tanh_input = gelu_coef * (preact + cubic_coef * preact * preact * preact)
    tangent = jnp.tanh(tanh_input)
    gelu_val = 0.5 * preact * (1.0 + tangent)
    slopes = 0.5 * (1.0 + tangent) + 0.5 * preact * (1.0 - tangent * tangent) * gelu_coef * (
        1.0 + 3.0 * cubic_coef * preact * preact
    )
    return (gelu_val, slopes)


def dispatch(row_ids, listed):
    match_table = (row_ids[:, None] == listed[None, :]).astype(jnp.int32)
    running = jnp.cumsum(match_table, axis=0) - 1
    slot_of = jnp.sum(match_table * jnp.arange(listed.shape[0], dtype=jnp.int32)[None, :], axis=1)
    within = jnp.sum(match_table * running, axis=1)
    return slot_of * CAP + within


def adam_step(params, moment_one, moment_two, gradient):
    moment_one = 0.9 * moment_one + 0.1 * gradient
    moment_two = 0.999 * moment_two + 0.001 * gradient * gradient
    correct_one = 1.0 - 0.9**10
    correct_two = 1.0 - 0.999**10
    updated = params - learn_rate * (moment_one / correct_one) / (
        jnp.sqrt(moment_two / correct_two) + 1e-08
    )
    return (updated.astype(jnp.bfloat16), moment_one, moment_two)


def sum_by_insertion(item_rows, arrived_grad, number):
    one_hot = (jnp.arange(number, dtype=jnp.int32)[:, None] == item_rows[None, :]).astype(
        arrived_grad.dtype
    )
    flat_grad = arrived_grad.reshape(item_rows.shape[0], -1)
    return jnp.dot(one_hot, flat_grad, preferred_element_type=jnp.float32)


def shards(signals, cotangent, row_insertion, touched, slot_map, weights, moment1, moment2):
    n_own = lax.axis_size("own")
    n_dp = lax.axis_size("dp")
    dp_at = lax.axis_index("dp")
    own_at = lax.axis_index("own")
    number = weights.shape[0]
    piece_rows = weights.shape[2]
    width_part = moment1.shape[3]
    pairs = n_dp * TOUCH
    stored = jnp.sum(
        jnp.where(
            touched[:, :, None] == jnp.arange(number, dtype=jnp.int32)[None, None, :],
            slot_map[None, None, :],
            0,
        ),
        axis=2,
    )
    peer_rows = stored.reshape(n_dp, n_own, TOUCH).transpose(1, 0, 2).reshape(-1)
    my_list = lax.dynamic_index_in_dim(touched, dp_at * n_own + own_at, 0, keepdims=False)
    places = dispatch(row_insertion, my_list)
    stacked = (
        jnp.zeros((TOUCH * CAP, 2 * SITES), signals.dtype)
        .at[places]
        .set(jnp.concatenate([signals, cotangent], axis=1))
    )
    stacked = lax.all_gather(stacked.reshape(TOUCH, CAP, 2 * SITES), "dp", axis=0, tiled=True)
    stacked = stacked.reshape(pairs, CAP, 2 * SITES)
    sig_slots = stacked[:, :, :SITES]
    cot_slots = stacked[:, :, SITES:]
    my_width = lax.dynamic_slice_in_dim(weights, dp_at * width_part, width_part, 3)
    pick = (peer_rows[:, None] == jnp.arange(number, dtype=jnp.int32)[None, :]).astype(weights.dtype)
    outgoing = jnp.dot(
        pick, my_width.reshape(number, -1), preferred_element_type=jnp.float32
    ).astype(weights.dtype)
    outgoing = outgoing.reshape(n_own, pairs, 2 * piece_rows * width_part)
    arrived = lax.all_to_all(outgoing, "own", split_axis=0, concat_axis=0, tiled=True)
    arrived = arrived.reshape(n_own, pairs, 2, piece_rows, width_part)
    arrived = arrived.transpose(1, 2, 0, 3, 4).reshape(pairs, 2, SITES, width_part)
    read_in = arrived[:, 0]
    read_out = arrived[:, 1]
    preact = jnp.einsum("kcs,ksw->kcw", sig_slots, read_in, preferred_element_type=jnp.float32)
    gelu_val, slopes = gelu_parts(preact)
    hidden = gelu_val.astype(jnp.bfloat16)
    pred_part = jnp.einsum("kcw,ksw->kcs", hidden, read_out, preferred_element_type=jnp.float32)
    back_hidden = jnp.einsum(
        "kcs,ksw->kcw", cot_slots, read_out, preferred_element_type=jnp.float32
    )
    back_pre = (back_hidden * slopes).astype(jnp.bfloat16)
    grad_in = jnp.einsum("kcs,kcw->ksw", sig_slots, back_pre, preferred_element_type=jnp.float32)
    grad_out = jnp.einsum("kcs,kcw->ksw", cot_slots, hidden, preferred_element_type=jnp.float32)
    grads = jnp.stack([grad_in, grad_out], axis=1).astype(jnp.bfloat16)
    pred_part, grads = lax.optimization_barrier((pred_part, grads))
    pred_slots = lax.psum_scatter(pred_part, "dp", scatter_dimension=0, tiled=True)
    pieces = grads.reshape(pairs, 2, n_own, piece_rows, width_part).transpose(2, 0, 1, 3, 4)
    pieces = pieces.reshape(n_own, pairs, 2 * piece_rows * width_part)
    arrived_grad = lax.all_to_all(pieces, "own", split_axis=0, concat_axis=0, tiled=True)
    arrived_grad, pred_slots = lax.optimization_barrier((arrived_grad, pred_slots))
    pred_slots = pred_slots.astype(jnp.bfloat16)
    table = sum_by_insertion(peer_rows, arrived_grad, number).reshape(
        number, 2, piece_rows, width_part
    )
    own_params = my_width.astype(jnp.float32)
    fresh_part, new_moment1, new_moment2 = adam_step(own_params, moment1, moment2, table)
    new_weights = lax.all_gather(fresh_part, "dp", axis=0, tiled=False)
    new_weights = new_weights.transpose(1, 2, 3, 0, 4).reshape(weights.shape)
    predicted = pred_slots.reshape(TOUCH * CAP, SITES)[places]
    return (predicted, new_weights, new_moment1, new_moment2)


def solution(mesh):
    in_specs = (
        P(("dp", "own"), None),
        P(("dp", "own"), None),
        P(("dp", "own")),
        P(),
        P(),
        P(None, None, "own", None),
        P(None, None, "own", "dp"),
        P(None, None, "own", "dp"),
    )
    out_specs = (
        P(("dp", "own"), None),
        P(None, None, "own", None),
        P(None, None, "own", "dp"),
        P(None, None, "own", "dp"),
    )
    return jax.shard_map(shards, mesh=mesh, in_specs=in_specs, out_specs=out_specs, check_vma=False)
```

```python
import functools
import math

import jax
import jax.numpy as jnp
from jax import lax
from jax.experimental import pallas as pl
from jax.experimental.pallas import tpu as pltpu
from jax.sharding import PartitionSpec as P

SITES = 384
WIDTH = 1024
TOUCH = 4
CAP = 128

MESH = pl.DeviceIdType.MESH

def _a2a_kernel(n_dp, n_own, full, x_ref, o_ref, send_sems, recv_sems, local_sem):
    dp_at = lax.axis_index("dp")
    own_at = lax.axis_index("own")
    if full:
        n = n_dp * n_own
        me = dp_at * n_own + own_at
        def dev(k):
            return (k // n_own, k % n_own)
    else:
        n = n_own
        me = own_at
        def dev(k):
            return (dp_at, k)
    barrier = pltpu.get_barrier_semaphore()

    def greet(i, c):
        peer = lax.rem(me + i, n)
        pl.semaphore_signal(barrier, 1, device_id=dev(peer), device_id_type=MESH)
        return c

    lax.fori_loop(1, n, greet, 0)
    pl.semaphore_wait(barrier, n - 1)
    local = pltpu.make_async_copy(x_ref.at[me], o_ref.at[me], local_sem)
    local.start()

    def send(i, c):
        peer = lax.rem(me + i, n)
        pltpu.make_async_remote_copy(
            src_ref=x_ref.at[peer], dst_ref=o_ref.at[me],
            send_sem=send_sems.at[peer], recv_sem=recv_sems.at[me],
            device_id=dev(peer), device_id_type=MESH,
        ).start()
        return c

    lax.fori_loop(1, n, send, 0)

    def finish(i, c):
        peer = lax.rem(me + i, n)
        src = lax.rem(me + n - i, n)
        pltpu.make_async_remote_copy(
            src_ref=x_ref.at[peer], dst_ref=o_ref.at[src],
            send_sem=send_sems.at[peer], recv_sem=recv_sems.at[src],
            device_id=dev(peer), device_id_type=MESH,
        ).wait_send()
        pltpu.make_async_remote_copy(
            src_ref=x_ref.at[peer], dst_ref=o_ref.at[src],
            send_sem=send_sems.at[peer], recv_sem=recv_sems.at[src],
            device_id=dev(src), device_id_type=MESH,
        ).wait_recv()
        return c

    lax.fori_loop(1, n, finish, 0)
    local.wait()


def exchange(x, n_dp, n_own, full, cid):
    n = x.shape[0]
    return pl.pallas_call(
        functools.partial(_a2a_kernel, n_dp, n_own, full),
        out_shape=jax.ShapeDtypeStruct(x.shape, x.dtype),
        in_specs=[pl.BlockSpec(memory_space=pl.ANY)],
        out_specs=pl.BlockSpec(memory_space=pl.ANY),
        scratch_shapes=[
            pltpu.SemaphoreType.DMA((n,)),
            pltpu.SemaphoreType.DMA((n,)),
            pltpu.SemaphoreType.DMA,
        ],
        compiler_params=pltpu.CompilerParams(collective_id=cid, has_side_effects=True),
    )(x)


gelu_coef = math.sqrt(2.0 / math.pi)
cubic_coef = 0.044715
learn_rate = 0.01
highest = lax.Precision.HIGHEST


def gelu_parts(preact):
    tanh_input = gelu_coef * (preact + cubic_coef * preact * preact * preact)
    tangent = jnp.tanh(tanh_input)
    gelu_val = 0.5 * preact * (1.0 + tangent)
    slopes = 0.5 * (1.0 + tangent) + 0.5 * preact * (1.0 - tangent * tangent) * gelu_coef * (
        1.0 + 3.0 * cubic_coef * preact * preact
    )
    return (gelu_val, slopes)


def dispatch(row_ids, listed):
    match_table = (row_ids[:, None] == listed[None, :]).astype(jnp.int32)
    running = jnp.cumsum(match_table, axis=0) - 1
    slot_of = jnp.sum(match_table * jnp.arange(listed.shape[0], dtype=jnp.int32)[None, :], axis=1)
    within = jnp.sum(match_table * running, axis=1)
    return slot_of * CAP + within


def adam_step(params, moment_one, moment_two, gradient):
    moment_one = 0.9 * moment_one + 0.1 * gradient
    moment_two = 0.999 * moment_two + 0.001 * gradient * gradient
    correct_one = 1.0 - 0.9**10
    correct_two = 1.0 - 0.999**10
    updated = params - learn_rate * (moment_one / correct_one) / (
        jnp.sqrt(moment_two / correct_two) + 1e-08
    )
    return (updated.astype(jnp.bfloat16), moment_one, moment_two)


def sum_by_insertion(item_rows, arrived_grad, number):
    one_hot = (jnp.arange(number, dtype=jnp.int32)[:, None] == item_rows[None, :]).astype(
        arrived_grad.dtype
    )
    flat_grad = arrived_grad.reshape(item_rows.shape[0], -1)
    return jnp.dot(one_hot, flat_grad, preferred_element_type=jnp.float32)


def shards(signals, cotangent, row_insertion, touched, slot_map, weights, moment1, moment2):
    n_own = lax.axis_size("own")
    n_dp = lax.axis_size("dp")
    dp_at = lax.axis_index("dp")
    own_at = lax.axis_index("own")
    number = weights.shape[0]
    piece_rows = weights.shape[2]
    width_part = moment1.shape[3]
    pairs = n_dp * TOUCH
    stored = jnp.sum(
        jnp.where(
            touched[:, :, None] == jnp.arange(number, dtype=jnp.int32)[None, None, :],
            slot_map[None, None, :],
            0,
        ),
        axis=2,
    )
    peer_rows = stored.reshape(n_dp, n_own, TOUCH).transpose(1, 0, 2).reshape(-1)
    my_list = lax.dynamic_index_in_dim(touched, dp_at * n_own + own_at, 0, keepdims=False)
    places = dispatch(row_insertion, my_list)
    stacked = (
        jnp.zeros((TOUCH * CAP, 2 * SITES), signals.dtype)
        .at[places]
        .set(jnp.concatenate([signals, cotangent], axis=1))
    )
    stacked = lax.all_gather(stacked.reshape(TOUCH, CAP, 2 * SITES), "dp", axis=0, tiled=True)
    stacked = stacked.reshape(pairs, CAP, 2 * SITES)
    sig_slots = stacked[:, :, :SITES]
    cot_slots = stacked[:, :, SITES:]
    my_width = lax.dynamic_slice_in_dim(weights, dp_at * width_part, width_part, 3)
    pick = (peer_rows[:, None] == jnp.arange(number, dtype=jnp.int32)[None, :]).astype(weights.dtype)
    outgoing = jnp.dot(
        pick, my_width.reshape(number, -1), preferred_element_type=jnp.float32
    ).astype(weights.dtype)
    outgoing = outgoing.reshape(n_own, pairs, 2 * piece_rows * width_part)
    item_rows = peer_rows.reshape(n_own, pairs)
    halves = 2
    half = pairs // halves
    pred_parts = []
    table = None
    fetched = [
        lax.all_to_all(
            outgoing[:, h * half : (h + 1) * half], "own", split_axis=0, concat_axis=0, tiled=True
        )
        for h in range(halves)
    ]
    sent = None
    for h in range(halves):
        chosen = slice(h * half, (h + 1) * half)
        arrived = fetched[h]
        arrived = arrived.reshape(n_own, half, 2, piece_rows, width_part)
        arrived = arrived.transpose(1, 2, 0, 3, 4).reshape(half, 2, SITES, width_part)
        read_in = arrived[:, 0]
        read_out = arrived[:, 1]
        sig_part = sig_slots[chosen]
        cot_part = cot_slots[chosen]
        preact = jnp.einsum("kcs,ksw->kcw", sig_part, read_in, preferred_element_type=jnp.float32)
        gelu_val, slopes = gelu_parts(preact)
        hidden = gelu_val.astype(jnp.bfloat16)
        pred_parts.append(
            jnp.einsum("kcw,ksw->kcs", hidden, read_out, preferred_element_type=jnp.float32)
        )
        back_hidden = jnp.einsum(
            "kcs,ksw->kcw", cot_part, read_out, preferred_element_type=jnp.float32
        )
        back_pre = (back_hidden * slopes).astype(jnp.bfloat16)
        grad_in = jnp.einsum("kcs,kcw->ksw", sig_part, back_pre, preferred_element_type=jnp.float32)
        grad_out = jnp.einsum("kcs,kcw->ksw", cot_part, hidden, preferred_element_type=jnp.float32)
        grads = jnp.stack([grad_in, grad_out], axis=1).astype(jnp.bfloat16)
        if h + 1 < halves:
            grads, fetched[h + 1] = lax.optimization_barrier((grads, fetched[h + 1]))
        if sent is not None:
            grads, sent = lax.optimization_barrier((grads, sent))
            table = sum_by_insertion(item_rows[:, :half].reshape(-1), sent, number)
        if h == halves - 1:
            pred_part = jnp.concatenate(pred_parts, axis=0)
            pred_part, grads = lax.optimization_barrier((pred_part, grads))
            pred_slots = lax.psum_scatter(pred_part, "dp", scatter_dimension=0, tiled=True)
        pieces = grads.reshape(half, 2, n_own, piece_rows, width_part).transpose(2, 0, 1, 3, 4)
        pieces = pieces.reshape(n_own, half, 2 * piece_rows * width_part)
        arrived_grad = lax.all_to_all(pieces, "own", split_axis=0, concat_axis=0, tiled=True)
        if h == halves - 1:
            arrived_grad, pred_slots = lax.optimization_barrier((arrived_grad, pred_slots))
            part = sum_by_insertion(item_rows[:, chosen].reshape(-1), arrived_grad, number)
            table = part + table
        else:
            sent = arrived_grad
    pred_slots = pred_slots.astype(jnp.bfloat16)
    table = table.reshape(number, 2, piece_rows, width_part)
    own_params = my_width.astype(jnp.float32)
    fresh_part, new_moment1, new_moment2 = adam_step(own_params, moment1, moment2, table)
    new_weights = lax.all_gather(fresh_part, "dp", axis=0, tiled=False)
    new_weights = new_weights.transpose(1, 2, 3, 0, 4).reshape(weights.shape)
    predicted = pred_slots.reshape(TOUCH * CAP, SITES)[places]
    return (predicted, new_weights, new_moment1, new_moment2)


def solution(mesh):
    in_specs = (
        P(("dp", "own"), None),
        P(("dp", "own"), None),
        P(("dp", "own")),
        P(),
        P(),
        P(None, None, "own", None),
        P(None, None, "own", "dp"),
        P(None, None, "own", "dp"),
    )
    out_specs = (
        P(("dp", "own"), None),
        P(None, None, "own", None),
        P(None, None, "own", "dp"),
        P(None, None, "own", "dp"),
    )
    return jax.shard_map(shards, mesh=mesh, in_specs=in_specs, out_specs=out_specs, check_vma=False)
```

```python
import functools
import math

import jax
import jax.numpy as jnp
from jax import lax
from jax.experimental import pallas as pl
from jax.experimental.pallas import tpu as pltpu
from jax.sharding import PartitionSpec as P

SITES = 384
WIDTH = 1024
TOUCH = 4
CAP = 128

MESH = pl.DeviceIdType.MESH

def _a2a_kernel(n_dp, n_own, full, x_ref, o_ref, send_sems, recv_sems, local_sem):
    dp_at = lax.axis_index("dp")
    own_at = lax.axis_index("own")
    if full:
        n = n_dp * n_own
        me = dp_at * n_own + own_at
        def dev(k):
            return (k // n_own, k % n_own)
    else:
        n = n_own
        me = own_at
        def dev(k):
            return (dp_at, k)
    barrier = pltpu.get_barrier_semaphore()

    def greet(i, c):
        peer = lax.rem(me + i, n)
        pl.semaphore_signal(barrier, 1, device_id=dev(peer), device_id_type=MESH)
        return c

    lax.fori_loop(1, n, greet, 0)
    pl.semaphore_wait(barrier, n - 1)
    local = pltpu.make_async_copy(x_ref.at[me], o_ref.at[me], local_sem)
    local.start()

    def send(i, c):
        peer = lax.rem(me + i, n)
        pltpu.make_async_remote_copy(
            src_ref=x_ref.at[peer], dst_ref=o_ref.at[me],
            send_sem=send_sems.at[peer], recv_sem=recv_sems.at[me],
            device_id=dev(peer), device_id_type=MESH,
        ).start()
        return c

    lax.fori_loop(1, n, send, 0)

    def finish(i, c):
        peer = lax.rem(me + i, n)
        src = lax.rem(me + n - i, n)
        pltpu.make_async_remote_copy(
            src_ref=x_ref.at[peer], dst_ref=o_ref.at[src],
            send_sem=send_sems.at[peer], recv_sem=recv_sems.at[src],
            device_id=dev(peer), device_id_type=MESH,
        ).wait_send()
        pltpu.make_async_remote_copy(
            src_ref=x_ref.at[peer], dst_ref=o_ref.at[src],
            send_sem=send_sems.at[peer], recv_sem=recv_sems.at[src],
            device_id=dev(src), device_id_type=MESH,
        ).wait_recv()
        return c

    lax.fori_loop(1, n, finish, 0)
    local.wait()


def exchange(x, n_dp, n_own, full, cid):
    n = x.shape[0]
    return pl.pallas_call(
        functools.partial(_a2a_kernel, n_dp, n_own, full),
        out_shape=jax.ShapeDtypeStruct(x.shape, x.dtype),
        in_specs=[pl.BlockSpec(memory_space=pl.ANY)],
        out_specs=pl.BlockSpec(memory_space=pl.ANY),
        scratch_shapes=[
            pltpu.SemaphoreType.DMA((n,)),
            pltpu.SemaphoreType.DMA((n,)),
            pltpu.SemaphoreType.DMA,
        ],
        compiler_params=pltpu.CompilerParams(collective_id=cid, has_side_effects=True),
    )(x)


gelu_coef = math.sqrt(2.0 / math.pi)
cubic_coef = 0.044715
learn_rate = 0.01
highest = lax.Precision.HIGHEST


def gelu_parts(preact):
    tanh_input = gelu_coef * (preact + cubic_coef * preact * preact * preact)
    tangent = jnp.tanh(tanh_input)
    gelu_val = 0.5 * preact * (1.0 + tangent)
    slopes = 0.5 * (1.0 + tangent) + 0.5 * preact * (1.0 - tangent * tangent) * gelu_coef * (
        1.0 + 3.0 * cubic_coef * preact * preact
    )
    return (gelu_val, slopes)


def dispatch(row_ids, listed):
    match_table = (row_ids[:, None] == listed[None, :]).astype(jnp.int32)
    running = jnp.cumsum(match_table, axis=0) - 1
    slot_of = jnp.sum(match_table * jnp.arange(listed.shape[0], dtype=jnp.int32)[None, :], axis=1)
    within = jnp.sum(match_table * running, axis=1)
    return slot_of * CAP + within


def adam_step(params, moment_one, moment_two, gradient):
    moment_one = 0.9 * moment_one + 0.1 * gradient
    moment_two = 0.999 * moment_two + 0.001 * gradient * gradient
    correct_one = 1.0 - 0.9**10
    correct_two = 1.0 - 0.999**10
    updated = params - learn_rate * (moment_one / correct_one) / (
        jnp.sqrt(moment_two / correct_two) + 1e-08
    )
    return (updated.astype(jnp.bfloat16), moment_one, moment_two)


def sum_by_insertion(item_rows, arrived_grad, number):
    one_hot = (jnp.arange(number, dtype=jnp.int32)[:, None] == item_rows[None, :]).astype(
        arrived_grad.dtype
    )
    flat_grad = arrived_grad.reshape(item_rows.shape[0], -1)
    return jnp.dot(one_hot, flat_grad, preferred_element_type=jnp.float32)


def shards(signals, cotangent, row_insertion, touched, slot_map, weights, moment1, moment2):
    n_own = lax.axis_size("own")
    n_dp = lax.axis_size("dp")
    dp_at = lax.axis_index("dp")
    own_at = lax.axis_index("own")
    number = weights.shape[0]
    piece_rows = weights.shape[2]
    width_part = moment1.shape[3]
    pairs = n_dp * TOUCH
    stored = jnp.sum(
        jnp.where(
            touched[:, :, None] == jnp.arange(number, dtype=jnp.int32)[None, None, :],
            slot_map[None, None, :],
            0,
        ),
        axis=2,
    )
    peer_rows = stored.reshape(n_dp, n_own, TOUCH).transpose(1, 0, 2).reshape(-1)
    my_list = lax.dynamic_index_in_dim(touched, dp_at * n_own + own_at, 0, keepdims=False)
    places = dispatch(row_insertion, my_list)
    stacked = (
        jnp.zeros((TOUCH * CAP, 2 * SITES), signals.dtype)
        .at[places]
        .set(jnp.concatenate([signals, cotangent], axis=1))
    )
    stacked = lax.all_gather(stacked.reshape(TOUCH, CAP, 2 * SITES), "dp", axis=0, tiled=True)
    stacked = stacked.reshape(pairs, CAP, 2 * SITES)
    sig_slots = stacked[:, :, :SITES]
    cot_slots = stacked[:, :, SITES:]
    my_width = lax.dynamic_slice_in_dim(weights, dp_at * width_part, width_part, 3)
    pick = (peer_rows[:, None] == jnp.arange(number, dtype=jnp.int32)[None, :]).astype(weights.dtype)
    outgoing = jnp.dot(
        pick, my_width.reshape(number, -1), preferred_element_type=jnp.float32
    ).astype(weights.dtype)
    chunks = TOUCH
    per = TOUCH // chunks
    part_pairs = n_dp * per
    flat = 2 * piece_rows * width_part
    item_rows = peer_rows.reshape(n_own, n_dp, chunks, per)
    sig_all = sig_slots.reshape(n_dp, chunks, per, CAP, SITES)
    cot_all = cot_slots.reshape(n_dp, chunks, per, CAP, SITES)
    fetched = lax.all_to_all(
        outgoing.reshape(n_own, pairs, flat), "own", split_axis=0, concat_axis=0, tiled=True
    )
    fetched = fetched.reshape(n_own, n_dp, chunks, per, flat)
    sent = None
    pieces = None
    table = None
    pred_chunks = []
    for c in range(chunks):
        taken = fetched[:, :, c]
        if pieces is not None:
            taken, pieces = lax.optimization_barrier((taken, pieces))
            sent = lax.all_to_all(pieces, "own", split_axis=0, concat_axis=0, tiled=True)
        arrived = taken.reshape(n_own, part_pairs, 2, piece_rows, width_part)
        arrived = arrived.transpose(1, 2, 0, 3, 4).reshape(part_pairs, 2, SITES, width_part)
        read_in = arrived[:, 0]
        read_out = arrived[:, 1]
        sig_part = sig_all[:, c].reshape(part_pairs, CAP, SITES)
        cot_part = cot_all[:, c].reshape(part_pairs, CAP, SITES)
        preact = jnp.einsum("kcs,ksw->kcw", sig_part, read_in, preferred_element_type=jnp.float32)
        gelu_val, slopes = gelu_parts(preact)
        hidden = gelu_val.astype(jnp.bfloat16)
        pred_part = jnp.einsum("kcw,ksw->kcs", hidden, read_out, preferred_element_type=jnp.float32)
        back_hidden = jnp.einsum(
            "kcs,ksw->kcw", cot_part, read_out, preferred_element_type=jnp.float32
        )
        back_pre = (back_hidden * slopes).astype(jnp.bfloat16)
        grad_in = jnp.einsum("kcs,kcw->ksw", sig_part, back_pre, preferred_element_type=jnp.float32)
        grad_out = jnp.einsum("kcs,kcw->ksw", cot_part, hidden, preferred_element_type=jnp.float32)
        grads = jnp.stack([grad_in, grad_out], axis=1).astype(jnp.bfloat16)
        pred_part, grads = lax.optimization_barrier((pred_part, grads))
        pred_chunks.append(lax.psum_scatter(pred_part, "dp", scatter_dimension=0, tiled=True))
        if sent is not None:
            grads, sent = lax.optimization_barrier((grads, sent))
            part = sum_by_insertion(item_rows[:, :, c - 1].reshape(-1), sent, number)
            table = part if table is None else table + part
        pieces = grads.reshape(part_pairs, 2, n_own, piece_rows, width_part)
        pieces = pieces.transpose(2, 0, 1, 3, 4).reshape(n_own, part_pairs, flat)
    sent = lax.all_to_all(pieces, "own", split_axis=0, concat_axis=0, tiled=True)
    part = sum_by_insertion(item_rows[:, :, chunks - 1].reshape(-1), sent, number)
    table = part if table is None else table + part
    pred_slots = jnp.stack(pred_chunks, axis=1).reshape(TOUCH, CAP, SITES).astype(jnp.bfloat16)
    table = table.reshape(number, 2, piece_rows, width_part)
    own_params = my_width.astype(jnp.float32)
    fresh_part, new_moment1, new_moment2 = adam_step(own_params, moment1, moment2, table)
    new_weights = lax.all_gather(fresh_part, "dp", axis=0, tiled=False)
    new_weights = new_weights.transpose(1, 2, 3, 0, 4).reshape(weights.shape)
    predicted = pred_slots.reshape(TOUCH * CAP, SITES)[places]
    return (predicted, new_weights, new_moment1, new_moment2)


def solution(mesh):
    in_specs = (
        P(("dp", "own"), None),
        P(("dp", "own"), None),
        P(("dp", "own")),
        P(),
        P(),
        P(None, None, "own", None),
        P(None, None, "own", "dp"),
        P(None, None, "own", "dp"),
    )
    out_specs = (
        P(("dp", "own"), None),
        P(None, None, "own", None),
        P(None, None, "own", "dp"),
        P(None, None, "own", "dp"),
    )
    return jax.shard_map(shards, mesh=mesh, in_specs=in_specs, out_specs=out_specs, check_vma=False)
```

```python
import functools
import math

import jax
import jax.numpy as jnp
from jax import lax
from jax.experimental import pallas as pl
from jax.experimental.pallas import tpu as pltpu
from jax.sharding import PartitionSpec as P

SITES = 384
WIDTH = 1024
TOUCH = 4
CAP = 128

MESH = pl.DeviceIdType.MESH

def _gather_kernel(n, x_ref, o_ref, send_sems, recv_sems, local_sem):
    me = lax.axis_index("dp")
    own_at = lax.axis_index("own")
    barrier = pltpu.get_barrier_semaphore()

    def greet(i, c):
        peer = lax.rem(me + i, n)
        pl.semaphore_signal(barrier, 1, device_id=(peer, own_at), device_id_type=MESH)
        return c

    lax.fori_loop(1, n, greet, 0)
    pl.semaphore_wait(barrier, n - 1)
    local = pltpu.make_async_copy(x_ref, o_ref.at[me], local_sem)
    local.start()

    def send(i, c):
        peer = lax.rem(me + i, n)
        pltpu.make_async_remote_copy(
            src_ref=x_ref, dst_ref=o_ref.at[me],
            send_sem=send_sems.at[peer], recv_sem=recv_sems.at[me],
            device_id=(peer, own_at), device_id_type=MESH,
        ).start()
        return c

    lax.fori_loop(1, n, send, 0)

    def finish(i, c):
        peer = lax.rem(me + i, n)
        src = lax.rem(me + n - i, n)
        pltpu.make_async_remote_copy(
            src_ref=x_ref, dst_ref=o_ref.at[src],
            send_sem=send_sems.at[peer], recv_sem=recv_sems.at[src],
            device_id=(peer, own_at), device_id_type=MESH,
        ).wait_send()
        pltpu.make_async_remote_copy(
            src_ref=x_ref, dst_ref=o_ref.at[src],
            send_sem=send_sems.at[peer], recv_sem=recv_sems.at[src],
            device_id=(src, own_at), device_id_type=MESH,
        ).wait_recv()
        return c

    lax.fori_loop(1, n, finish, 0)
    local.wait()


def gather_dp(x, n, cid):
    return pl.pallas_call(
        functools.partial(_gather_kernel, n),
        out_shape=jax.ShapeDtypeStruct((n,) + x.shape, x.dtype),
        in_specs=[pl.BlockSpec(memory_space=pl.ANY)],
        out_specs=pl.BlockSpec(memory_space=pl.ANY),
        scratch_shapes=[
            pltpu.SemaphoreType.DMA((n,)),
            pltpu.SemaphoreType.DMA((n,)),
            pltpu.SemaphoreType.DMA,
        ],
        compiler_params=pltpu.CompilerParams(collective_id=cid, has_side_effects=True),
    )(x)


gelu_coef = math.sqrt(2.0 / math.pi)
cubic_coef = 0.044715
learn_rate = 0.01
highest = lax.Precision.HIGHEST


def gelu_parts(preact):
    tanh_input = gelu_coef * (preact + cubic_coef * preact * preact * preact)
    tangent = jnp.tanh(tanh_input)
    gelu_val = 0.5 * preact * (1.0 + tangent)
    slopes = 0.5 * (1.0 + tangent) + 0.5 * preact * (1.0 - tangent * tangent) * gelu_coef * (
        1.0 + 3.0 * cubic_coef * preact * preact
    )
    return (gelu_val, slopes)


def dispatch(row_ids, listed):
    match_table = (row_ids[:, None] == listed[None, :]).astype(jnp.int32)
    running = jnp.cumsum(match_table, axis=0) - 1
    slot_of = jnp.sum(match_table * jnp.arange(listed.shape[0], dtype=jnp.int32)[None, :], axis=1)
    within = jnp.sum(match_table * running, axis=1)
    return slot_of * CAP + within


def adam_step(params, moment_one, moment_two, gradient):
    moment_one = 0.9 * moment_one + 0.1 * gradient
    moment_two = 0.999 * moment_two + 0.001 * gradient * gradient
    correct_one = 1.0 - 0.9**10
    correct_two = 1.0 - 0.999**10
    updated = params - learn_rate * (moment_one / correct_one) / (
        jnp.sqrt(moment_two / correct_two) + 1e-08
    )
    return (updated.astype(jnp.bfloat16), moment_one, moment_two)


def sum_by_insertion(item_rows, arrived_grad, number):
    one_hot = (jnp.arange(number, dtype=jnp.int32)[:, None] == item_rows[None, :]).astype(
        arrived_grad.dtype
    )
    flat_grad = arrived_grad.reshape(item_rows.shape[0], -1)
    return jnp.dot(one_hot, flat_grad, preferred_element_type=jnp.float32)


def shards(signals, cotangent, row_insertion, touched, slot_map, weights, moment1, moment2):
    n_own = lax.axis_size("own")
    n_dp = lax.axis_size("dp")
    dp_at = lax.axis_index("dp")
    own_at = lax.axis_index("own")
    number = weights.shape[0]
    piece_rows = weights.shape[2]
    width_part = moment1.shape[3]
    pairs = n_dp * TOUCH
    stored = jnp.sum(
        jnp.where(
            touched[:, :, None] == jnp.arange(number, dtype=jnp.int32)[None, None, :],
            slot_map[None, None, :],
            0,
        ),
        axis=2,
    )
    peer_rows = stored.reshape(n_dp, n_own, TOUCH).transpose(1, 0, 2).reshape(-1)
    my_list = lax.dynamic_index_in_dim(touched, dp_at * n_own + own_at, 0, keepdims=False)
    places = dispatch(row_insertion, my_list)
    stacked = (
        jnp.zeros((TOUCH * CAP, 2 * SITES), signals.dtype)
        .at[places]
        .set(jnp.concatenate([signals, cotangent], axis=1))
    )
    stacked = lax.all_gather(stacked.reshape(TOUCH, CAP, 2 * SITES), "dp", axis=0, tiled=True)
    stacked = stacked.reshape(pairs, CAP, 2 * SITES)
    sig_slots = stacked[:, :, :SITES]
    cot_slots = stacked[:, :, SITES:]
    my_width = lax.dynamic_slice_in_dim(weights, dp_at * width_part, width_part, 3)
    pick = (peer_rows[:, None] == jnp.arange(number, dtype=jnp.int32)[None, :]).astype(weights.dtype)
    outgoing = jnp.dot(
        pick, my_width.reshape(number, -1), preferred_element_type=jnp.float32
    ).astype(weights.dtype)
    outgoing = outgoing.reshape(n_own, pairs, 2 * piece_rows * width_part)
    item_rows = peer_rows.reshape(n_own, pairs)
    halves = 2
    half = pairs // halves
    pred_parts = []
    table = None
    fetched = [
        lax.all_to_all(
            outgoing[:, h * half : (h + 1) * half], "own", split_axis=0, concat_axis=0, tiled=True
        )
        for h in range(halves)
    ]
    sent = None
    for h in range(halves):
        chosen = slice(h * half, (h + 1) * half)
        arrived = fetched[h]
        arrived = arrived.reshape(n_own, half, 2, piece_rows, width_part)
        arrived = arrived.transpose(1, 2, 0, 3, 4).reshape(half, 2, SITES, width_part)
        read_in = arrived[:, 0]
        read_out = arrived[:, 1]
        sig_part = sig_slots[chosen]
        cot_part = cot_slots[chosen]
        preact = jnp.einsum("kcs,ksw->kcw", sig_part, read_in, preferred_element_type=jnp.float32)
        gelu_val, slopes = gelu_parts(preact)
        hidden = gelu_val.astype(jnp.bfloat16)
        pred_parts.append(
            jnp.einsum("kcw,ksw->kcs", hidden, read_out, preferred_element_type=jnp.float32)
        )
        back_hidden = jnp.einsum(
            "kcs,ksw->kcw", cot_part, read_out, preferred_element_type=jnp.float32
        )
        back_pre = (back_hidden * slopes).astype(jnp.bfloat16)
        grad_in = jnp.einsum("kcs,kcw->ksw", sig_part, back_pre, preferred_element_type=jnp.float32)
        grad_out = jnp.einsum("kcs,kcw->ksw", cot_part, hidden, preferred_element_type=jnp.float32)
        grads = jnp.stack([grad_in, grad_out], axis=1).astype(jnp.bfloat16)
        if h + 1 < halves:
            grads, fetched[h + 1] = lax.optimization_barrier((grads, fetched[h + 1]))
        if sent is not None:
            grads, sent = lax.optimization_barrier((grads, sent))
            table = sum_by_insertion(item_rows[:, :half].reshape(-1), sent, number)
        if h == halves - 1:
            pred_part = jnp.concatenate(pred_parts, axis=0)
            pred_part, grads = lax.optimization_barrier((pred_part, grads))
            pred_slots = lax.psum_scatter(pred_part, "dp", scatter_dimension=0, tiled=True)
        pieces = grads.reshape(half, 2, n_own, piece_rows, width_part).transpose(2, 0, 1, 3, 4)
        pieces = pieces.reshape(n_own, half, 2 * piece_rows * width_part)
        arrived_grad = lax.all_to_all(pieces, "own", split_axis=0, concat_axis=0, tiled=True)
        if h == halves - 1:
            arrived_grad, pred_slots = lax.optimization_barrier((arrived_grad, pred_slots))
            part = sum_by_insertion(item_rows[:, chosen].reshape(-1), arrived_grad, number)
            table = part + table
        else:
            sent = arrived_grad
    pred_slots = pred_slots.astype(jnp.bfloat16)
    table = table.reshape(number, 2, piece_rows, width_part)
    own_params = my_width.astype(jnp.float32)
    fresh_part, new_moment1, new_moment2 = adam_step(own_params, moment1, moment2, table)
    new_weights = gather_dp(fresh_part, n_dp, 0)
    new_weights = new_weights.transpose(1, 2, 3, 0, 4).reshape(weights.shape)
    predicted = pred_slots.reshape(TOUCH * CAP, SITES)[places]
    return (predicted, new_weights, new_moment1, new_moment2)


def solution(mesh):
    in_specs = (
        P(("dp", "own"), None),
        P(("dp", "own"), None),
        P(("dp", "own")),
        P(),
        P(),
        P(None, None, "own", None),
        P(None, None, "own", "dp"),
        P(None, None, "own", "dp"),
    )
    out_specs = (
        P(("dp", "own"), None),
        P(None, None, "own", None),
        P(None, None, "own", "dp"),
        P(None, None, "own", "dp"),
    )
    return jax.shard_map(shards, mesh=mesh, in_specs=in_specs, out_specs=out_specs, check_vma=False)
```

```python
import functools
import math

import jax
import jax.numpy as jnp
from jax import lax
from jax.experimental import pallas as pl
from jax.experimental.pallas import tpu as pltpu
from jax.sharding import PartitionSpec as P

SITES = 384
WIDTH = 1024
TOUCH = 4
CAP = 128

MESH = pl.DeviceIdType.MESH

def _a2a_kernel(n_dp, n_own, full, x_ref, o_ref, send_sems, recv_sems, local_sem):
    dp_at = lax.axis_index("dp")
    own_at = lax.axis_index("own")
    if full:
        n = n_dp * n_own
        me = dp_at * n_own + own_at
        def dev(k):
            return (k // n_own, k % n_own)
    else:
        n = n_own
        me = own_at
        def dev(k):
            return (dp_at, k)
    barrier = pltpu.get_barrier_semaphore()

    def greet(i, c):
        peer = lax.rem(me + i, n)
        pl.semaphore_signal(barrier, 1, device_id=dev(peer), device_id_type=MESH)
        return c

    lax.fori_loop(1, n, greet, 0)
    pl.semaphore_wait(barrier, n - 1)
    local = pltpu.make_async_copy(x_ref.at[me], o_ref.at[me], local_sem)
    local.start()

    def send(i, c):
        peer = lax.rem(me + i, n)
        pltpu.make_async_remote_copy(
            src_ref=x_ref.at[peer], dst_ref=o_ref.at[me],
            send_sem=send_sems.at[peer], recv_sem=recv_sems.at[me],
            device_id=dev(peer), device_id_type=MESH,
        ).start()
        return c

    lax.fori_loop(1, n, send, 0)

    def finish(i, c):
        peer = lax.rem(me + i, n)
        src = lax.rem(me + n - i, n)
        pltpu.make_async_remote_copy(
            src_ref=x_ref.at[peer], dst_ref=o_ref.at[src],
            send_sem=send_sems.at[peer], recv_sem=recv_sems.at[src],
            device_id=dev(peer), device_id_type=MESH,
        ).wait_send()
        pltpu.make_async_remote_copy(
            src_ref=x_ref.at[peer], dst_ref=o_ref.at[src],
            send_sem=send_sems.at[peer], recv_sem=recv_sems.at[src],
            device_id=dev(src), device_id_type=MESH,
        ).wait_recv()
        return c

    lax.fori_loop(1, n, finish, 0)
    local.wait()


def exchange(x, n_dp, n_own, full, cid):
    n = x.shape[0]
    return pl.pallas_call(
        functools.partial(_a2a_kernel, n_dp, n_own, full),
        out_shape=jax.ShapeDtypeStruct(x.shape, x.dtype),
        in_specs=[pl.BlockSpec(memory_space=pl.ANY)],
        out_specs=pl.BlockSpec(memory_space=pl.ANY),
        scratch_shapes=[
            pltpu.SemaphoreType.DMA((n,)),
            pltpu.SemaphoreType.DMA((n,)),
            pltpu.SemaphoreType.DMA,
        ],
        compiler_params=pltpu.CompilerParams(collective_id=cid, has_side_effects=True),
    )(x)


gelu_coef = math.sqrt(2.0 / math.pi)
cubic_coef = 0.044715
learn_rate = 0.01
highest = lax.Precision.HIGHEST


def gelu_parts(preact):
    tanh_input = gelu_coef * (preact + cubic_coef * preact * preact * preact)
    tangent = jnp.tanh(tanh_input)
    gelu_val = 0.5 * preact * (1.0 + tangent)
    slopes = 0.5 * (1.0 + tangent) + 0.5 * preact * (1.0 - tangent * tangent) * gelu_coef * (
        1.0 + 3.0 * cubic_coef * preact * preact
    )
    return (gelu_val, slopes)


def dispatch(row_ids, listed):
    match_table = (row_ids[:, None] == listed[None, :]).astype(jnp.int32)
    running = jnp.cumsum(match_table, axis=0) - 1
    slot_of = jnp.sum(match_table * jnp.arange(listed.shape[0], dtype=jnp.int32)[None, :], axis=1)
    within = jnp.sum(match_table * running, axis=1)
    return slot_of * CAP + within


def adam_step(params, moment_one, moment_two, gradient):
    moment_one = 0.9 * moment_one + 0.1 * gradient
    moment_two = 0.999 * moment_two + 0.001 * gradient * gradient
    correct_one = 1.0 - 0.9**10
    correct_two = 1.0 - 0.999**10
    updated = params - learn_rate * (moment_one / correct_one) / (
        jnp.sqrt(moment_two / correct_two) + 1e-08
    )
    return (updated.astype(jnp.bfloat16), moment_one, moment_two)


def sum_by_insertion(item_rows, arrived_grad, number):
    one_hot = (jnp.arange(number, dtype=jnp.int32)[:, None] == item_rows[None, :]).astype(
        arrived_grad.dtype
    )
    flat_grad = arrived_grad.reshape(item_rows.shape[0], -1)
    return jnp.dot(one_hot, flat_grad, preferred_element_type=jnp.float32)


def shards(signals, cotangent, row_insertion, touched, slot_map, weights, moment1, moment2):
    n_own = lax.axis_size("own")
    n_dp = lax.axis_size("dp")
    dp_at = lax.axis_index("dp")
    own_at = lax.axis_index("own")
    number = weights.shape[0]
    piece_rows = weights.shape[2]
    width_part = moment1.shape[3]
    pairs = n_dp * TOUCH
    stored = jnp.sum(
        jnp.where(
            touched[:, :, None] == jnp.arange(number, dtype=jnp.int32)[None, None, :],
            slot_map[None, None, :],
            0,
        ),
        axis=2,
    )
    peer_rows = stored.reshape(n_dp, n_own, TOUCH).transpose(1, 0, 2).reshape(-1)
    my_list = lax.dynamic_index_in_dim(touched, dp_at * n_own + own_at, 0, keepdims=False)
    places = dispatch(row_insertion, my_list)
    stacked = (
        jnp.zeros((TOUCH * CAP, 2 * SITES), signals.dtype)
        .at[places]
        .set(jnp.concatenate([signals, cotangent], axis=1))
    )
    stacked = lax.all_gather(stacked.reshape(TOUCH, CAP, 2 * SITES), "dp", axis=0, tiled=True)
    stacked = stacked.reshape(pairs, CAP, 2 * SITES)
    sig_slots = stacked[:, :, :SITES]
    cot_slots = stacked[:, :, SITES:]
    my_width = lax.dynamic_slice_in_dim(weights, dp_at * width_part, width_part, 3)
    pick = (peer_rows[:, None] == jnp.arange(number, dtype=jnp.int32)[None, :]).astype(weights.dtype)
    outgoing = jnp.dot(
        pick, my_width.reshape(number, -1), preferred_element_type=jnp.float32
    ).astype(weights.dtype)
    outgoing = outgoing.reshape(n_own, pairs, 2 * piece_rows * width_part)
    item_rows = peer_rows.reshape(n_own, pairs)
    halves = 2
    half = pairs // halves
    pred_parts = []
    table = None
    fetched = [
        lax.all_to_all(
            outgoing[:, h * half : (h + 1) * half], "own", split_axis=0, concat_axis=0, tiled=True
        )
        for h in range(halves)
    ]
    sent = None
    for h in range(halves):
        chosen = slice(h * half, (h + 1) * half)
        arrived = fetched[h]
        arrived = arrived.reshape(n_own, half, 2, piece_rows, width_part)
        arrived = arrived.transpose(1, 2, 0, 3, 4).reshape(half, 2, SITES, width_part)
        read_in = arrived[:, 0]
        read_out = arrived[:, 1]
        sig_part = sig_slots[chosen]
        cot_part = cot_slots[chosen]
        preact = jnp.einsum("kcs,ksw->kcw", sig_part, read_in, preferred_element_type=jnp.float32)
        gelu_val, slopes = gelu_parts(preact)
        hidden = gelu_val.astype(jnp.bfloat16)
        pred_parts.append(
            jnp.einsum("kcw,ksw->kcs", hidden, read_out, preferred_element_type=jnp.float32)
        )
        back_hidden = jnp.einsum(
            "kcs,ksw->kcw", cot_part, read_out, preferred_element_type=jnp.float32
        )
        back_pre = (back_hidden * slopes).astype(jnp.bfloat16)
        grad_in = jnp.einsum("kcs,kcw->ksw", sig_part, back_pre, preferred_element_type=jnp.float32)
        grad_out = jnp.einsum("kcs,kcw->ksw", cot_part, hidden, preferred_element_type=jnp.float32)
        grads = jnp.stack([grad_in, grad_out], axis=1).astype(jnp.bfloat16)
        if h + 1 < halves:
            grads, fetched[h + 1] = lax.optimization_barrier((grads, fetched[h + 1]))
        if sent is not None:
            grads, sent = lax.optimization_barrier((grads, sent))
            table = sum_by_insertion(item_rows[:, :half].reshape(-1), sent, number)
        if h == halves - 1:
            pred_part = jnp.concatenate(pred_parts, axis=0)
            pred_part, grads = lax.optimization_barrier((pred_part, grads))
            pred_slots = lax.psum_scatter(
                pred_part.astype(jnp.bfloat16), "dp", scatter_dimension=0, tiled=True
            )
        pieces = grads.reshape(half, 2, n_own, piece_rows, width_part).transpose(2, 0, 1, 3, 4)
        pieces = pieces.reshape(n_own, half, 2 * piece_rows * width_part)
        arrived_grad = lax.all_to_all(pieces, "own", split_axis=0, concat_axis=0, tiled=True)
        if h == halves - 1:
            arrived_grad, pred_slots = lax.optimization_barrier((arrived_grad, pred_slots))
            part = sum_by_insertion(item_rows[:, chosen].reshape(-1), arrived_grad, number)
            table = part + table
        else:
            sent = arrived_grad
    pred_slots = pred_slots.astype(jnp.bfloat16)
    table = table.reshape(number, 2, piece_rows, width_part)
    own_params = my_width.astype(jnp.float32)
    fresh_part, new_moment1, new_moment2 = adam_step(own_params, moment1, moment2, table)
    new_weights = lax.all_gather(fresh_part, "dp", axis=0, tiled=False)
    new_weights = new_weights.transpose(1, 2, 3, 0, 4).reshape(weights.shape)
    predicted = pred_slots.reshape(TOUCH * CAP, SITES)[places]
    return (predicted, new_weights, new_moment1, new_moment2)


def solution(mesh):
    in_specs = (
        P(("dp", "own"), None),
        P(("dp", "own"), None),
        P(("dp", "own")),
        P(),
        P(),
        P(None, None, "own", None),
        P(None, None, "own", "dp"),
        P(None, None, "own", "dp"),
    )
    out_specs = (
        P(("dp", "own"), None),
        P(None, None, "own", None),
        P(None, None, "own", "dp"),
        P(None, None, "own", "dp"),
    )
    return jax.shard_map(shards, mesh=mesh, in_specs=in_specs, out_specs=out_specs, check_vma=False)
```

```python
import functools
import math

import jax
import jax.numpy as jnp
from jax import lax
from jax.experimental import pallas as pl
from jax.experimental.pallas import tpu as pltpu
from jax.sharding import PartitionSpec as P

SITES = 384
WIDTH = 1024
TOUCH = 4
CAP = 128

MESH = pl.DeviceIdType.MESH

def _a2a_kernel(n_dp, n_own, full, x_ref, o_ref, send_sems, recv_sems, local_sem):
    dp_at = lax.axis_index("dp")
    own_at = lax.axis_index("own")
    if full:
        n = n_dp * n_own
        me = dp_at * n_own + own_at
        def dev(k):
            return (k // n_own, k % n_own)
    else:
        n = n_own
        me = own_at
        def dev(k):
            return (dp_at, k)
    barrier = pltpu.get_barrier_semaphore()

    def greet(i, c):
        peer = lax.rem(me + i, n)
        pl.semaphore_signal(barrier, 1, device_id=dev(peer), device_id_type=MESH)
        return c

    lax.fori_loop(1, n, greet, 0)
    pl.semaphore_wait(barrier, n - 1)
    local = pltpu.make_async_copy(x_ref.at[me], o_ref.at[me], local_sem)
    local.start()

    def send(i, c):
        peer = lax.rem(me + i, n)
        pltpu.make_async_remote_copy(
            src_ref=x_ref.at[peer], dst_ref=o_ref.at[me],
            send_sem=send_sems.at[peer], recv_sem=recv_sems.at[me],
            device_id=dev(peer), device_id_type=MESH,
        ).start()
        return c

    lax.fori_loop(1, n, send, 0)

    def finish(i, c):
        peer = lax.rem(me + i, n)
        src = lax.rem(me + n - i, n)
        pltpu.make_async_remote_copy(
            src_ref=x_ref.at[peer], dst_ref=o_ref.at[src],
            send_sem=send_sems.at[peer], recv_sem=recv_sems.at[src],
            device_id=dev(peer), device_id_type=MESH,
        ).wait_send()
        pltpu.make_async_remote_copy(
            src_ref=x_ref.at[peer], dst_ref=o_ref.at[src],
            send_sem=send_sems.at[peer], recv_sem=recv_sems.at[src],
            device_id=dev(src), device_id_type=MESH,
        ).wait_recv()
        return c

    lax.fori_loop(1, n, finish, 0)
    local.wait()


def exchange(x, n_dp, n_own, full, cid):
    n = x.shape[0]
    return pl.pallas_call(
        functools.partial(_a2a_kernel, n_dp, n_own, full),
        out_shape=jax.ShapeDtypeStruct(x.shape, x.dtype),
        in_specs=[pl.BlockSpec(memory_space=pl.ANY)],
        out_specs=pl.BlockSpec(memory_space=pl.ANY),
        scratch_shapes=[
            pltpu.SemaphoreType.DMA((n,)),
            pltpu.SemaphoreType.DMA((n,)),
            pltpu.SemaphoreType.DMA,
        ],
        compiler_params=pltpu.CompilerParams(collective_id=cid, has_side_effects=True),
    )(x)


gelu_coef = math.sqrt(2.0 / math.pi)
cubic_coef = 0.044715
learn_rate = 0.01
highest = lax.Precision.HIGHEST


def gelu_parts(preact):
    tanh_input = gelu_coef * (preact + cubic_coef * preact * preact * preact)
    tangent = jnp.tanh(tanh_input)
    gelu_val = 0.5 * preact * (1.0 + tangent)
    slopes = 0.5 * (1.0 + tangent) + 0.5 * preact * (1.0 - tangent * tangent) * gelu_coef * (
        1.0 + 3.0 * cubic_coef * preact * preact
    )
    return (gelu_val, slopes)


def dispatch(row_ids, listed):
    match_table = (row_ids[:, None] == listed[None, :]).astype(jnp.int32)
    running = jnp.cumsum(match_table, axis=0) - 1
    slot_of = jnp.sum(match_table * jnp.arange(listed.shape[0], dtype=jnp.int32)[None, :], axis=1)
    within = jnp.sum(match_table * running, axis=1)
    return slot_of * CAP + within


def adam_step(params, moment_one, moment_two, gradient):
    moment_one = 0.9 * moment_one + 0.1 * gradient
    moment_two = 0.999 * moment_two + 0.001 * gradient * gradient
    correct_one = 1.0 - 0.9**10
    correct_two = 1.0 - 0.999**10
    updated = params - learn_rate * (moment_one / correct_one) / (
        jnp.sqrt(moment_two / correct_two) + 1e-08
    )
    return (updated.astype(jnp.bfloat16), moment_one, moment_two)


def sum_by_insertion(item_rows, arrived_grad, number):
    one_hot = (jnp.arange(number, dtype=jnp.int32)[:, None] == item_rows[None, :]).astype(
        arrived_grad.dtype
    )
    flat_grad = arrived_grad.reshape(item_rows.shape[0], -1)
    return jnp.dot(one_hot, flat_grad, preferred_element_type=jnp.float32)


def shards(signals, cotangent, row_insertion, touched, slot_map, weights, moment1, moment2):
    n_own = lax.axis_size("own")
    n_dp = lax.axis_size("dp")
    dp_at = lax.axis_index("dp")
    own_at = lax.axis_index("own")
    number = weights.shape[0]
    piece_rows = weights.shape[2]
    width_part = moment1.shape[3]
    pairs = n_dp * TOUCH
    stored = jnp.sum(
        jnp.where(
            touched[:, :, None] == jnp.arange(number, dtype=jnp.int32)[None, None, :],
            slot_map[None, None, :],
            0,
        ),
        axis=2,
    )
    peer_rows = stored.reshape(n_dp, n_own, TOUCH).transpose(1, 0, 2).reshape(-1)
    my_list = lax.dynamic_index_in_dim(touched, dp_at * n_own + own_at, 0, keepdims=False)
    places = dispatch(row_insertion, my_list)
    peer_places = lax.all_gather(places, "dp", axis=0, tiled=False)
    stacked = (
        jnp.zeros((TOUCH * CAP, 2 * SITES), signals.dtype)
        .at[places]
        .set(jnp.concatenate([signals, cotangent], axis=1))
    )
    stacked = lax.all_gather(stacked.reshape(TOUCH, CAP, 2 * SITES), "dp", axis=0, tiled=True)
    stacked = stacked.reshape(pairs, CAP, 2 * SITES)
    sig_slots = stacked[:, :, :SITES]
    cot_slots = stacked[:, :, SITES:]
    my_width = lax.dynamic_slice_in_dim(weights, dp_at * width_part, width_part, 3)
    pick = (peer_rows[:, None] == jnp.arange(number, dtype=jnp.int32)[None, :]).astype(weights.dtype)
    outgoing = jnp.dot(
        pick, my_width.reshape(number, -1), preferred_element_type=jnp.float32
    ).astype(weights.dtype)
    outgoing = outgoing.reshape(n_own, pairs, 2 * piece_rows * width_part)
    item_rows = peer_rows.reshape(n_own, pairs)
    halves = 2
    half = pairs // halves
    pred_parts = []
    table = None
    fetched = [
        lax.all_to_all(
            outgoing[:, h * half : (h + 1) * half], "own", split_axis=0, concat_axis=0, tiled=True
        )
        for h in range(halves)
    ]
    sent = None
    for h in range(halves):
        chosen = slice(h * half, (h + 1) * half)
        arrived = fetched[h]
        arrived = arrived.reshape(n_own, half, 2, piece_rows, width_part)
        arrived = arrived.transpose(1, 2, 0, 3, 4).reshape(half, 2, SITES, width_part)
        read_in = arrived[:, 0]
        read_out = arrived[:, 1]
        sig_part = sig_slots[chosen]
        cot_part = cot_slots[chosen]
        preact = jnp.einsum("kcs,ksw->kcw", sig_part, read_in, preferred_element_type=jnp.float32)
        gelu_val, slopes = gelu_parts(preact)
        hidden = gelu_val.astype(jnp.bfloat16)
        pred_parts.append(
            jnp.einsum("kcw,ksw->kcs", hidden, read_out, preferred_element_type=jnp.float32)
        )
        back_hidden = jnp.einsum(
            "kcs,ksw->kcw", cot_part, read_out, preferred_element_type=jnp.float32
        )
        back_pre = (back_hidden * slopes).astype(jnp.bfloat16)
        grad_in = jnp.einsum("kcs,kcw->ksw", sig_part, back_pre, preferred_element_type=jnp.float32)
        grad_out = jnp.einsum("kcs,kcw->ksw", cot_part, hidden, preferred_element_type=jnp.float32)
        grads = jnp.stack([grad_in, grad_out], axis=1).astype(jnp.bfloat16)
        if h + 1 < halves:
            grads, fetched[h + 1] = lax.optimization_barrier((grads, fetched[h + 1]))
        if sent is not None:
            grads, sent = lax.optimization_barrier((grads, sent))
            table = sum_by_insertion(item_rows[:, :half].reshape(-1), sent, number)
        if h == halves - 1:
            pred_part = jnp.concatenate(pred_parts, axis=0)
            pred_part, grads = lax.optimization_barrier((pred_part, grads))
            pred_part = pred_part.reshape(n_dp, TOUCH * CAP, SITES)
            real_rows = jnp.take_along_axis(pred_part, peer_places[:, :, None], axis=1)
            pred_slots = lax.psum_scatter(real_rows, "dp", scatter_dimension=0, tiled=True)
        pieces = grads.reshape(half, 2, n_own, piece_rows, width_part).transpose(2, 0, 1, 3, 4)
        pieces = pieces.reshape(n_own, half, 2 * piece_rows * width_part)
        arrived_grad = lax.all_to_all(pieces, "own", split_axis=0, concat_axis=0, tiled=True)
        if h == halves - 1:
            arrived_grad, pred_slots = lax.optimization_barrier((arrived_grad, pred_slots))
            part = sum_by_insertion(item_rows[:, chosen].reshape(-1), arrived_grad, number)
            table = part + table
        else:
            sent = arrived_grad
    pred_slots = pred_slots.astype(jnp.bfloat16)
    table = table.reshape(number, 2, piece_rows, width_part)
    own_params = my_width.astype(jnp.float32)
    fresh_part, new_moment1, new_moment2 = adam_step(own_params, moment1, moment2, table)
    new_weights = lax.all_gather(fresh_part, "dp", axis=0, tiled=False)
    new_weights = new_weights.transpose(1, 2, 3, 0, 4).reshape(weights.shape)
    predicted = pred_slots.reshape(-1, SITES)
    return (predicted, new_weights, new_moment1, new_moment2)


def solution(mesh):
    in_specs = (
        P(("dp", "own"), None),
        P(("dp", "own"), None),
        P(("dp", "own")),
        P(),
        P(),
        P(None, None, "own", None),
        P(None, None, "own", "dp"),
        P(None, None, "own", "dp"),
    )
    out_specs = (
        P(("dp", "own"), None),
        P(None, None, "own", None),
        P(None, None, "own", "dp"),
        P(None, None, "own", "dp"),
    )
    return jax.shard_map(shards, mesh=mesh, in_specs=in_specs, out_specs=out_specs, check_vma=False)
```

```python
import functools
import math

import jax
import jax.numpy as jnp
from jax import lax
from jax.experimental import pallas as pl
from jax.experimental.pallas import tpu as pltpu
from jax.sharding import PartitionSpec as P

SITES = 384
WIDTH = 1024
TOUCH = 4
CAP = 128

MESH = pl.DeviceIdType.MESH

def _a2a_kernel(n_dp, n_own, full, x_ref, o_ref, send_sems, recv_sems, local_sem):
    dp_at = lax.axis_index("dp")
    own_at = lax.axis_index("own")
    if full:
        n = n_dp * n_own
        me = dp_at * n_own + own_at
        def dev(k):
            return (k // n_own, k % n_own)
    else:
        n = n_own
        me = own_at
        def dev(k):
            return (dp_at, k)
    barrier = pltpu.get_barrier_semaphore()

    def greet(i, c):
        peer = lax.rem(me + i, n)
        pl.semaphore_signal(barrier, 1, device_id=dev(peer), device_id_type=MESH)
        return c

    lax.fori_loop(1, n, greet, 0)
    pl.semaphore_wait(barrier, n - 1)
    local = pltpu.make_async_copy(x_ref.at[me], o_ref.at[me], local_sem)
    local.start()

    def send(i, c):
        peer = lax.rem(me + i, n)
        pltpu.make_async_remote_copy(
            src_ref=x_ref.at[peer], dst_ref=o_ref.at[me],
            send_sem=send_sems.at[peer], recv_sem=recv_sems.at[me],
            device_id=dev(peer), device_id_type=MESH,
        ).start()
        return c

    lax.fori_loop(1, n, send, 0)

    def finish(i, c):
        peer = lax.rem(me + i, n)
        src = lax.rem(me + n - i, n)
        pltpu.make_async_remote_copy(
            src_ref=x_ref.at[peer], dst_ref=o_ref.at[src],
            send_sem=send_sems.at[peer], recv_sem=recv_sems.at[src],
            device_id=dev(peer), device_id_type=MESH,
        ).wait_send()
        pltpu.make_async_remote_copy(
            src_ref=x_ref.at[peer], dst_ref=o_ref.at[src],
            send_sem=send_sems.at[peer], recv_sem=recv_sems.at[src],
            device_id=dev(src), device_id_type=MESH,
        ).wait_recv()
        return c

    lax.fori_loop(1, n, finish, 0)
    local.wait()


def exchange(x, n_dp, n_own, full, cid):
    n = x.shape[0]
    return pl.pallas_call(
        functools.partial(_a2a_kernel, n_dp, n_own, full),
        out_shape=jax.ShapeDtypeStruct(x.shape, x.dtype),
        in_specs=[pl.BlockSpec(memory_space=pl.ANY)],
        out_specs=pl.BlockSpec(memory_space=pl.ANY),
        scratch_shapes=[
            pltpu.SemaphoreType.DMA((n,)),
            pltpu.SemaphoreType.DMA((n,)),
            pltpu.SemaphoreType.DMA,
        ],
        compiler_params=pltpu.CompilerParams(collective_id=cid, has_side_effects=True),
    )(x)


gelu_coef = math.sqrt(2.0 / math.pi)
cubic_coef = 0.044715
learn_rate = 0.01
highest = lax.Precision.HIGHEST


def gelu_parts(preact):
    tanh_input = gelu_coef * (preact + cubic_coef * preact * preact * preact)
    tangent = jnp.tanh(tanh_input)
    gelu_val = 0.5 * preact * (1.0 + tangent)
    slopes = 0.5 * (1.0 + tangent) + 0.5 * preact * (1.0 - tangent * tangent) * gelu_coef * (
        1.0 + 3.0 * cubic_coef * preact * preact
    )
    return (gelu_val, slopes)


def dispatch(row_ids, listed):
    match_table = (row_ids[:, None] == listed[None, :]).astype(jnp.int32)
    running = jnp.cumsum(match_table, axis=0) - 1
    slot_of = jnp.sum(match_table * jnp.arange(listed.shape[0], dtype=jnp.int32)[None, :], axis=1)
    within = jnp.sum(match_table * running, axis=1)
    return slot_of * CAP + within


def adam_step(params, moment_one, moment_two, gradient):
    moment_one = 0.9 * moment_one + 0.1 * gradient
    moment_two = 0.999 * moment_two + 0.001 * gradient * gradient
    correct_one = 1.0 - 0.9**10
    correct_two = 1.0 - 0.999**10
    updated = params - learn_rate * (moment_one / correct_one) / (
        jnp.sqrt(moment_two / correct_two) + 1e-08
    )
    return (updated.astype(jnp.bfloat16), moment_one, moment_two)


def sum_by_insertion(item_rows, arrived_grad, number):
    one_hot = (jnp.arange(number, dtype=jnp.int32)[:, None] == item_rows[None, :]).astype(
        arrived_grad.dtype
    )
    flat_grad = arrived_grad.reshape(item_rows.shape[0], -1)
    return jnp.dot(one_hot, flat_grad, preferred_element_type=jnp.float32)


def shards(signals, cotangent, row_insertion, touched, slot_map, weights, moment1, moment2):
    n_own = lax.axis_size("own")
    n_dp = lax.axis_size("dp")
    dp_at = lax.axis_index("dp")
    own_at = lax.axis_index("own")
    number = weights.shape[0]
    piece_rows = weights.shape[2]
    width_part = moment1.shape[3]
    pairs = n_dp * TOUCH
    stored = jnp.sum(
        jnp.where(
            touched[:, :, None] == jnp.arange(number, dtype=jnp.int32)[None, None, :],
            slot_map[None, None, :],
            0,
        ),
        axis=2,
    )
    peer_rows = stored.reshape(n_dp, n_own, TOUCH).transpose(1, 0, 2).reshape(-1)
    my_list = lax.dynamic_index_in_dim(touched, dp_at * n_own + own_at, 0, keepdims=False)
    places = dispatch(row_insertion, my_list)
    row_of_slot = (
        jnp.full((TOUCH * CAP,), -1, jnp.int32)
        .at[places]
        .set(jnp.arange(places.shape[0], dtype=jnp.int32))
        .astype(signals.dtype)
    )
    stacked = (
        jnp.zeros((TOUCH * CAP, 2 * SITES), signals.dtype)
        .at[places]
        .set(jnp.concatenate([signals, cotangent], axis=1))
    )
    extra = jnp.zeros((16, 2 * SITES), signals.dtype).at[0, : TOUCH * CAP].set(row_of_slot)
    gathered = lax.all_gather(
        jnp.concatenate([stacked, extra], axis=0), "dp", axis=0, tiled=False
    )
    stacked = gathered[:, : TOUCH * CAP]
    peer_slots = gathered[:, TOUCH * CAP, : TOUCH * CAP].astype(jnp.int32)
    stacked = stacked.reshape(pairs, CAP, 2 * SITES)
    sig_slots = stacked[:, :, :SITES]
    cot_slots = stacked[:, :, SITES:]
    my_width = lax.dynamic_slice_in_dim(weights, dp_at * width_part, width_part, 3)
    pick = (peer_rows[:, None] == jnp.arange(number, dtype=jnp.int32)[None, :]).astype(weights.dtype)
    outgoing = jnp.dot(
        pick, my_width.reshape(number, -1), preferred_element_type=jnp.float32
    ).astype(weights.dtype)
    outgoing = outgoing.reshape(n_own, pairs, 2 * piece_rows * width_part)
    item_rows = peer_rows.reshape(n_own, pairs)
    halves = 2
    half = pairs // halves
    pred_parts = []
    table = None
    fetched = [
        lax.all_to_all(
            outgoing[:, h * half : (h + 1) * half], "own", split_axis=0, concat_axis=0, tiled=True
        )
        for h in range(halves)
    ]
    sent = None
    for h in range(halves):
        chosen = slice(h * half, (h + 1) * half)
        arrived = fetched[h]
        arrived = arrived.reshape(n_own, half, 2, piece_rows, width_part)
        arrived = arrived.transpose(1, 2, 0, 3, 4).reshape(half, 2, SITES, width_part)
        read_in = arrived[:, 0]
        read_out = arrived[:, 1]
        sig_part = sig_slots[chosen]
        cot_part = cot_slots[chosen]
        preact = jnp.einsum("kcs,ksw->kcw", sig_part, read_in, preferred_element_type=jnp.float32)
        gelu_val, slopes = gelu_parts(preact)
        hidden = gelu_val.astype(jnp.bfloat16)
        pred_parts.append(
            jnp.einsum("kcw,ksw->kcs", hidden, read_out, preferred_element_type=jnp.float32)
        )
        back_hidden = jnp.einsum(
            "kcs,ksw->kcw", cot_part, read_out, preferred_element_type=jnp.float32
        )
        back_pre = (back_hidden * slopes).astype(jnp.bfloat16)
        grad_in = jnp.einsum("kcs,kcw->ksw", sig_part, back_pre, preferred_element_type=jnp.float32)
        grad_out = jnp.einsum("kcs,kcw->ksw", cot_part, hidden, preferred_element_type=jnp.float32)
        grads = jnp.stack([grad_in, grad_out], axis=1).astype(jnp.bfloat16)
        if h + 1 < halves:
            grads, fetched[h + 1] = lax.optimization_barrier((grads, fetched[h + 1]))
        if sent is not None:
            grads, sent = lax.optimization_barrier((grads, sent))
            table = sum_by_insertion(item_rows[:, :half].reshape(-1), sent, number)
        if h == halves - 1:
            pred_part = jnp.concatenate(pred_parts, axis=0)
            pred_part, grads = lax.optimization_barrier((pred_part, grads))
            pred_part = pred_part.reshape(n_dp, TOUCH * CAP, SITES)
            choose = (
                peer_slots[:, None, :]
                == jnp.arange(signals.shape[0], dtype=jnp.int32)[None, :, None]
            ).astype(jnp.float32)
            real_rows = jnp.einsum(
                "qrs,qsx->qrx", choose, pred_part, precision=highest,
                preferred_element_type=jnp.float32,
            )
            pred_slots = lax.psum_scatter(real_rows, "dp", scatter_dimension=0, tiled=True)
        pieces = grads.reshape(half, 2, n_own, piece_rows, width_part).transpose(2, 0, 1, 3, 4)
        pieces = pieces.reshape(n_own, half, 2 * piece_rows * width_part)
        arrived_grad = lax.all_to_all(pieces, "own", split_axis=0, concat_axis=0, tiled=True)
        if h == halves - 1:
            arrived_grad, pred_slots = lax.optimization_barrier((arrived_grad, pred_slots))
            part = sum_by_insertion(item_rows[:, chosen].reshape(-1), arrived_grad, number)
            table = part + table
        else:
            sent = arrived_grad
    pred_slots = pred_slots.astype(jnp.bfloat16)
    table = table.reshape(number, 2, piece_rows, width_part)
    own_params = my_width.astype(jnp.float32)
    fresh_part, new_moment1, new_moment2 = adam_step(own_params, moment1, moment2, table)
    new_weights = lax.all_gather(fresh_part, "dp", axis=0, tiled=False)
    new_weights = new_weights.transpose(1, 2, 3, 0, 4).reshape(weights.shape)
    predicted = pred_slots.reshape(-1, SITES)
    return (predicted, new_weights, new_moment1, new_moment2)


def solution(mesh):
    in_specs = (
        P(("dp", "own"), None),
        P(("dp", "own"), None),
        P(("dp", "own")),
        P(),
        P(),
        P(None, None, "own", None),
        P(None, None, "own", "dp"),
        P(None, None, "own", "dp"),
    )
    out_specs = (
        P(("dp", "own"), None),
        P(None, None, "own", None),
        P(None, None, "own", "dp"),
        P(None, None, "own", "dp"),
    )
    return jax.shard_map(shards, mesh=mesh, in_specs=in_specs, out_specs=out_specs, check_vma=False)
```

```python
import functools
import math

import jax
import jax.numpy as jnp
from jax import lax
from jax.experimental import pallas as pl
from jax.experimental.pallas import tpu as pltpu
from jax.sharding import PartitionSpec as P

SITES = 384
WIDTH = 1024
TOUCH = 4
CAP = 128

MESH = pl.DeviceIdType.MESH

def _a2a_kernel(n_dp, n_own, full, x_ref, o_ref, send_sems, recv_sems, local_sem):
    dp_at = lax.axis_index("dp")
    own_at = lax.axis_index("own")
    if full:
        n = n_dp * n_own
        me = dp_at * n_own + own_at
        def dev(k):
            return (k // n_own, k % n_own)
    else:
        n = n_own
        me = own_at
        def dev(k):
            return (dp_at, k)
    barrier = pltpu.get_barrier_semaphore()

    def greet(i, c):
        peer = lax.rem(me + i, n)
        pl.semaphore_signal(barrier, 1, device_id=dev(peer), device_id_type=MESH)
        return c

    lax.fori_loop(1, n, greet, 0)
    pl.semaphore_wait(barrier, n - 1)
    local = pltpu.make_async_copy(x_ref.at[me], o_ref.at[me], local_sem)
    local.start()

    def send(i, c):
        peer = lax.rem(me + i, n)
        pltpu.make_async_remote_copy(
            src_ref=x_ref.at[peer], dst_ref=o_ref.at[me],
            send_sem=send_sems.at[peer], recv_sem=recv_sems.at[me],
            device_id=dev(peer), device_id_type=MESH,
        ).start()
        return c

    lax.fori_loop(1, n, send, 0)

    def finish(i, c):
        peer = lax.rem(me + i, n)
        src = lax.rem(me + n - i, n)
        pltpu.make_async_remote_copy(
            src_ref=x_ref.at[peer], dst_ref=o_ref.at[src],
            send_sem=send_sems.at[peer], recv_sem=recv_sems.at[src],
            device_id=dev(peer), device_id_type=MESH,
        ).wait_send()
        pltpu.make_async_remote_copy(
            src_ref=x_ref.at[peer], dst_ref=o_ref.at[src],
            send_sem=send_sems.at[peer], recv_sem=recv_sems.at[src],
            device_id=dev(src), device_id_type=MESH,
        ).wait_recv()
        return c

    lax.fori_loop(1, n, finish, 0)
    local.wait()


def exchange(x, n_dp, n_own, full, cid):
    n = x.shape[0]
    return pl.pallas_call(
        functools.partial(_a2a_kernel, n_dp, n_own, full),
        out_shape=jax.ShapeDtypeStruct(x.shape, x.dtype),
        in_specs=[pl.BlockSpec(memory_space=pl.ANY)],
        out_specs=pl.BlockSpec(memory_space=pl.ANY),
        scratch_shapes=[
            pltpu.SemaphoreType.DMA((n,)),
            pltpu.SemaphoreType.DMA((n,)),
            pltpu.SemaphoreType.DMA,
        ],
        compiler_params=pltpu.CompilerParams(collective_id=cid, has_side_effects=True),
    )(x)


gelu_coef = math.sqrt(2.0 / math.pi)
cubic_coef = 0.044715
learn_rate = 0.01
highest = lax.Precision.HIGHEST


def gelu_parts(preact):
    tanh_input = gelu_coef * (preact + cubic_coef * preact * preact * preact)
    tangent = jnp.tanh(tanh_input)
    gelu_val = 0.5 * preact * (1.0 + tangent)
    slopes = 0.5 * (1.0 + tangent) + 0.5 * preact * (1.0 - tangent * tangent) * gelu_coef * (
        1.0 + 3.0 * cubic_coef * preact * preact
    )
    return (gelu_val, slopes)


def dispatch(row_ids, listed):
    match_table = (row_ids[:, None] == listed[None, :]).astype(jnp.int32)
    running = jnp.cumsum(match_table, axis=0) - 1
    slot_of = jnp.sum(match_table * jnp.arange(listed.shape[0], dtype=jnp.int32)[None, :], axis=1)
    within = jnp.sum(match_table * running, axis=1)
    return slot_of * CAP + within


def adam_step(params, moment_one, moment_two, gradient):
    moment_one = 0.9 * moment_one + 0.1 * gradient
    moment_two = 0.999 * moment_two + 0.001 * gradient * gradient
    correct_one = 1.0 - 0.9**10
    correct_two = 1.0 - 0.999**10
    updated = params - learn_rate * (moment_one / correct_one) / (
        jnp.sqrt(moment_two / correct_two) + 1e-08
    )
    return (updated.astype(jnp.bfloat16), moment_one, moment_two)


def sum_by_insertion(item_rows, arrived_grad, number):
    one_hot = (jnp.arange(number, dtype=jnp.int32)[:, None] == item_rows[None, :]).astype(
        arrived_grad.dtype
    )
    flat_grad = arrived_grad.reshape(item_rows.shape[0], -1)
    return jnp.dot(one_hot, flat_grad, preferred_element_type=jnp.float32)


def shards(signals, cotangent, row_insertion, touched, slot_map, weights, moment1, moment2):
    n_own = lax.axis_size("own")
    n_dp = lax.axis_size("dp")
    dp_at = lax.axis_index("dp")
    own_at = lax.axis_index("own")
    number = weights.shape[0]
    piece_rows = weights.shape[2]
    width_part = moment1.shape[3]
    pairs = n_dp * TOUCH
    stored = jnp.sum(
        jnp.where(
            touched[:, :, None] == jnp.arange(number, dtype=jnp.int32)[None, None, :],
            slot_map[None, None, :],
            0,
        ),
        axis=2,
    )
    peer_rows = stored.reshape(n_dp, n_own, TOUCH).transpose(1, 0, 2).reshape(-1)
    my_list = lax.dynamic_index_in_dim(touched, dp_at * n_own + own_at, 0, keepdims=False)
    places = dispatch(row_insertion, my_list)
    row_of_slot = (
        jnp.full((TOUCH * CAP,), -1, jnp.int32)
        .at[places]
        .set(jnp.arange(places.shape[0], dtype=jnp.int32))
        .astype(signals.dtype)
    )
    stacked = (
        jnp.zeros((TOUCH * CAP, 2 * SITES), signals.dtype)
        .at[places]
        .set(jnp.concatenate([signals, cotangent], axis=1))
    )
    extra = jnp.zeros((16, 2 * SITES), signals.dtype).at[0, : TOUCH * CAP].set(row_of_slot)
    gathered = lax.all_gather(
        jnp.concatenate([stacked, extra], axis=0), "dp", axis=0, tiled=False
    )
    stacked = gathered[:, : TOUCH * CAP]
    peer_slots = gathered[:, TOUCH * CAP, : TOUCH * CAP].astype(jnp.int32)
    stacked = stacked.reshape(pairs, CAP, 2 * SITES)
    sig_slots = stacked[:, :, :SITES]
    cot_slots = stacked[:, :, SITES:]
    my_width = lax.dynamic_slice_in_dim(weights, dp_at * width_part, width_part, 3)
    pick = (peer_rows[:, None] == jnp.arange(number, dtype=jnp.int32)[None, :]).astype(weights.dtype)
    outgoing = jnp.dot(
        pick, my_width.reshape(number, -1), preferred_element_type=jnp.float32
    ).astype(weights.dtype)
    outgoing = outgoing.reshape(n_own, pairs, 2 * piece_rows * width_part)
    item_rows = peer_rows.reshape(n_own, pairs)
    halves = 4
    half = pairs // halves
    pred_parts = []
    table = None
    fetched = [
        lax.all_to_all(
            outgoing[:, h * half : (h + 1) * half], "own", split_axis=0, concat_axis=0, tiled=True
        )
        for h in range(halves)
    ]
    sent = None
    for h in range(halves):
        chosen = slice(h * half, (h + 1) * half)
        arrived = fetched[h]
        arrived = arrived.reshape(n_own, half, 2, piece_rows, width_part)
        arrived = arrived.transpose(1, 2, 0, 3, 4).reshape(half, 2, SITES, width_part)
        read_in = arrived[:, 0]
        read_out = arrived[:, 1]
        sig_part = sig_slots[chosen]
        cot_part = cot_slots[chosen]
        preact = jnp.einsum("kcs,ksw->kcw", sig_part, read_in, preferred_element_type=jnp.float32)
        gelu_val, slopes = gelu_parts(preact)
        hidden = gelu_val.astype(jnp.bfloat16)
        pred_parts.append(
            jnp.einsum("kcw,ksw->kcs", hidden, read_out, preferred_element_type=jnp.float32)
        )
        back_hidden = jnp.einsum(
            "kcs,ksw->kcw", cot_part, read_out, preferred_element_type=jnp.float32
        )
        back_pre = (back_hidden * slopes).astype(jnp.bfloat16)
        grad_in = jnp.einsum("kcs,kcw->ksw", sig_part, back_pre, preferred_element_type=jnp.float32)
        grad_out = jnp.einsum("kcs,kcw->ksw", cot_part, hidden, preferred_element_type=jnp.float32)
        grads = jnp.stack([grad_in, grad_out], axis=1).astype(jnp.bfloat16)
        if h + 1 < halves:
            grads, fetched[h + 1] = lax.optimization_barrier((grads, fetched[h + 1]))
        if sent is not None:
            grads, sent = lax.optimization_barrier((grads, sent))
            part = sum_by_insertion(
                item_rows[:, (h - 1) * half : h * half].reshape(-1), sent, number
            )
            table = part if table is None else table + part
        if h == halves - 1:
            pred_part = jnp.concatenate(pred_parts, axis=0)
            pred_part, grads = lax.optimization_barrier((pred_part, grads))
            pred_part = pred_part.reshape(n_dp, TOUCH * CAP, SITES)
            choose = (
                peer_slots[:, None, :]
                == jnp.arange(signals.shape[0], dtype=jnp.int32)[None, :, None]
            ).astype(jnp.float32)
            real_rows = jnp.einsum(
                "qrs,qsx->qrx", choose, pred_part, precision=highest,
                preferred_element_type=jnp.float32,
            )
            pred_slots = lax.psum_scatter(real_rows, "dp", scatter_dimension=0, tiled=True)
        pieces = grads.reshape(half, 2, n_own, piece_rows, width_part).transpose(2, 0, 1, 3, 4)
        pieces = pieces.reshape(n_own, half, 2 * piece_rows * width_part)
        arrived_grad = lax.all_to_all(pieces, "own", split_axis=0, concat_axis=0, tiled=True)
        if h == halves - 1:
            arrived_grad, pred_slots = lax.optimization_barrier((arrived_grad, pred_slots))
            part = sum_by_insertion(item_rows[:, chosen].reshape(-1), arrived_grad, number)
            table = part + table
        else:
            sent = arrived_grad
    pred_slots = pred_slots.astype(jnp.bfloat16)
    table = table.reshape(number, 2, piece_rows, width_part)
    own_params = my_width.astype(jnp.float32)
    fresh_part, new_moment1, new_moment2 = adam_step(own_params, moment1, moment2, table)
    new_weights = lax.all_gather(fresh_part, "dp", axis=0, tiled=False)
    new_weights = new_weights.transpose(1, 2, 3, 0, 4).reshape(weights.shape)
    predicted = pred_slots.reshape(-1, SITES)
    return (predicted, new_weights, new_moment1, new_moment2)


def solution(mesh):
    in_specs = (
        P(("dp", "own"), None),
        P(("dp", "own"), None),
        P(("dp", "own")),
        P(),
        P(),
        P(None, None, "own", None),
        P(None, None, "own", "dp"),
        P(None, None, "own", "dp"),
    )
    out_specs = (
        P(("dp", "own"), None),
        P(None, None, "own", None),
        P(None, None, "own", "dp"),
        P(None, None, "own", "dp"),
    )
    return jax.shard_map(shards, mesh=mesh, in_specs=in_specs, out_specs=out_specs, check_vma=False)
```

```python
import functools
import math

import jax
import jax.numpy as jnp
from jax import lax
from jax.experimental import pallas as pl
from jax.experimental.pallas import tpu as pltpu
from jax.sharding import PartitionSpec as P

SITES = 384
WIDTH = 1024
TOUCH = 4
CAP = 128

MESH = pl.DeviceIdType.MESH

def _a2a_kernel(n_dp, n_own, full, x_ref, o_ref, send_sems, recv_sems, local_sem):
    dp_at = lax.axis_index("dp")
    own_at = lax.axis_index("own")
    if full:
        n = n_dp * n_own
        me = dp_at * n_own + own_at
        def dev(k):
            return (k // n_own, k % n_own)
    else:
        n = n_own
        me = own_at
        def dev(k):
            return (dp_at, k)
    barrier = pltpu.get_barrier_semaphore()

    def greet(i, c):
        peer = lax.rem(me + i, n)
        pl.semaphore_signal(barrier, 1, device_id=dev(peer), device_id_type=MESH)
        return c

    lax.fori_loop(1, n, greet, 0)
    pl.semaphore_wait(barrier, n - 1)
    local = pltpu.make_async_copy(x_ref.at[me], o_ref.at[me], local_sem)
    local.start()

    def send(i, c):
        peer = lax.rem(me + i, n)
        pltpu.make_async_remote_copy(
            src_ref=x_ref.at[peer], dst_ref=o_ref.at[me],
            send_sem=send_sems.at[peer], recv_sem=recv_sems.at[me],
            device_id=dev(peer), device_id_type=MESH,
        ).start()
        return c

    lax.fori_loop(1, n, send, 0)

    def finish(i, c):
        peer = lax.rem(me + i, n)
        src = lax.rem(me + n - i, n)
        pltpu.make_async_remote_copy(
            src_ref=x_ref.at[peer], dst_ref=o_ref.at[src],
            send_sem=send_sems.at[peer], recv_sem=recv_sems.at[src],
            device_id=dev(peer), device_id_type=MESH,
        ).wait_send()
        pltpu.make_async_remote_copy(
            src_ref=x_ref.at[peer], dst_ref=o_ref.at[src],
            send_sem=send_sems.at[peer], recv_sem=recv_sems.at[src],
            device_id=dev(src), device_id_type=MESH,
        ).wait_recv()
        return c

    lax.fori_loop(1, n, finish, 0)
    local.wait()


def exchange(x, n_dp, n_own, full, cid):
    n = x.shape[0]
    return pl.pallas_call(
        functools.partial(_a2a_kernel, n_dp, n_own, full),
        out_shape=jax.ShapeDtypeStruct(x.shape, x.dtype),
        in_specs=[pl.BlockSpec(memory_space=pl.ANY)],
        out_specs=pl.BlockSpec(memory_space=pl.ANY),
        scratch_shapes=[
            pltpu.SemaphoreType.DMA((n,)),
            pltpu.SemaphoreType.DMA((n,)),
            pltpu.SemaphoreType.DMA,
        ],
        compiler_params=pltpu.CompilerParams(collective_id=cid, has_side_effects=True),
    )(x)


gelu_coef = math.sqrt(2.0 / math.pi)
cubic_coef = 0.044715
learn_rate = 0.01
highest = lax.Precision.HIGHEST


def gelu_parts(preact):
    tanh_input = gelu_coef * (preact + cubic_coef * preact * preact * preact)
    tangent = jnp.tanh(tanh_input)
    gelu_val = 0.5 * preact * (1.0 + tangent)
    slopes = 0.5 * (1.0 + tangent) + 0.5 * preact * (1.0 - tangent * tangent) * gelu_coef * (
        1.0 + 3.0 * cubic_coef * preact * preact
    )
    return (gelu_val, slopes)


def dispatch(row_ids, listed):
    match_table = (row_ids[:, None] == listed[None, :]).astype(jnp.int32)
    running = jnp.cumsum(match_table, axis=0) - 1
    slot_of = jnp.sum(match_table * jnp.arange(listed.shape[0], dtype=jnp.int32)[None, :], axis=1)
    within = jnp.sum(match_table * running, axis=1)
    return slot_of * CAP + within


def adam_step(params, moment_one, moment_two, gradient):
    moment_one = 0.9 * moment_one + 0.1 * gradient
    moment_two = 0.999 * moment_two + 0.001 * gradient * gradient
    correct_one = 1.0 - 0.9**10
    correct_two = 1.0 - 0.999**10
    updated = params - learn_rate * (moment_one / correct_one) / (
        jnp.sqrt(moment_two / correct_two) + 1e-08
    )
    return (updated.astype(jnp.bfloat16), moment_one, moment_two)


def sum_by_insertion(item_rows, arrived_grad, number):
    one_hot = (jnp.arange(number, dtype=jnp.int32)[:, None] == item_rows[None, :]).astype(
        arrived_grad.dtype
    )
    flat_grad = arrived_grad.reshape(item_rows.shape[0], -1)
    return jnp.dot(one_hot, flat_grad, preferred_element_type=jnp.float32)


def shards(signals, cotangent, row_insertion, touched, slot_map, weights, moment1, moment2):
    n_own = lax.axis_size("own")
    n_dp = lax.axis_size("dp")
    dp_at = lax.axis_index("dp")
    own_at = lax.axis_index("own")
    number = weights.shape[0]
    piece_rows = weights.shape[2]
    width_part = moment1.shape[3]
    pairs = n_dp * TOUCH
    stored = jnp.sum(
        jnp.where(
            touched[:, :, None] == jnp.arange(number, dtype=jnp.int32)[None, None, :],
            slot_map[None, None, :],
            0,
        ),
        axis=2,
    )
    peer_rows = stored.reshape(n_dp, n_own, TOUCH).transpose(1, 0, 2).reshape(-1)
    my_list = lax.dynamic_index_in_dim(touched, dp_at * n_own + own_at, 0, keepdims=False)
    places = dispatch(row_insertion, my_list)
    row_of_slot = (
        jnp.full((TOUCH * CAP,), -1, jnp.int32)
        .at[places]
        .set(jnp.arange(places.shape[0], dtype=jnp.int32))
        .astype(signals.dtype)
    )
    stacked = (
        jnp.zeros((TOUCH * CAP, 2 * SITES), signals.dtype)
        .at[places]
        .set(jnp.concatenate([signals, cotangent], axis=1))
    )
    extra = jnp.zeros((16, 2 * SITES), signals.dtype).at[0, : TOUCH * CAP].set(row_of_slot)
    gathered = lax.all_gather(
        jnp.concatenate([stacked, extra], axis=0), "dp", axis=0, tiled=False
    )
    stacked = gathered[:, : TOUCH * CAP]
    peer_slots = gathered[:, TOUCH * CAP, : TOUCH * CAP].astype(jnp.int32)
    stacked = stacked.reshape(pairs, CAP, 2 * SITES)
    sig_slots = stacked[:, :, :SITES]
    cot_slots = stacked[:, :, SITES:]
    my_width = lax.dynamic_slice_in_dim(weights, dp_at * width_part, width_part, 3)
    pick = (peer_rows[:, None] == jnp.arange(number, dtype=jnp.int32)[None, :]).astype(weights.dtype)
    outgoing = jnp.dot(
        pick, my_width.reshape(number, -1), preferred_element_type=jnp.float32
    ).astype(weights.dtype)
    outgoing = outgoing.reshape(n_own, pairs, 2 * piece_rows * width_part)
    item_rows = peer_rows.reshape(n_own, pairs)
    halves = 2
    half = pairs // halves
    pred_parts = []
    table = None
    fetched = [
        lax.all_to_all(
            outgoing[:, h * half : (h + 1) * half], "own", split_axis=0, concat_axis=0, tiled=True
        )
        for h in range(halves)
    ]
    sent = None
    for h in range(halves):
        chosen = slice(h * half, (h + 1) * half)
        arrived = fetched[h]
        arrived = arrived.reshape(n_own, half, 2, piece_rows, width_part)
        arrived = arrived.transpose(1, 2, 0, 3, 4).reshape(half, 2, SITES, width_part)
        read_in = arrived[:, 0]
        read_out = arrived[:, 1]
        sig_part = sig_slots[chosen]
        cot_part = cot_slots[chosen]
        preact = jnp.einsum("kcs,ksw->kcw", sig_part, read_in, preferred_element_type=jnp.float32)
        gelu_val, slopes = gelu_parts(preact)
        hidden = gelu_val.astype(jnp.bfloat16)
        pred_parts.append(
            jnp.einsum("kcw,ksw->kcs", hidden, read_out, preferred_element_type=jnp.float32)
        )
        back_hidden = jnp.einsum(
            "kcs,ksw->kcw", cot_part, read_out, preferred_element_type=jnp.float32
        )
        back_pre = (back_hidden * slopes).astype(jnp.bfloat16)
        grad_in = jnp.einsum("kcs,kcw->ksw", sig_part, back_pre, preferred_element_type=jnp.float32)
        grad_out = jnp.einsum("kcs,kcw->ksw", cot_part, hidden, preferred_element_type=jnp.float32)
        grads = jnp.stack([grad_in, grad_out], axis=1).astype(jnp.bfloat16)
        if h + 1 < halves:
            grads, fetched[h + 1] = lax.optimization_barrier((grads, fetched[h + 1]))
        if sent is not None:
            grads, sent = lax.optimization_barrier((grads, sent))
            table = sum_by_insertion(item_rows[:, :half].reshape(-1), sent, number)
        if h == halves - 1:
            pred_part = jnp.concatenate(pred_parts, axis=0)
            pred_part, grads = lax.optimization_barrier((pred_part, grads))
            pred_part = pred_part.reshape(n_dp, TOUCH * CAP, SITES)
            choose = (
                peer_slots[:, None, :]
                == jnp.arange(signals.shape[0], dtype=jnp.int32)[None, :, None]
            ).astype(jnp.bfloat16)
            top = pred_part.astype(jnp.bfloat16)
            rest = pred_part - top.astype(jnp.float32)
            middle = rest.astype(jnp.bfloat16)
            low = (rest - middle.astype(jnp.float32)).astype(jnp.bfloat16)
            real_rows = None
            for piece in (top, middle, low):
                picked = jnp.einsum(
                    "qrs,qsx->qrx", choose, piece, preferred_element_type=jnp.float32
                )
                real_rows = picked if real_rows is None else real_rows + picked
            pred_slots = lax.psum_scatter(real_rows, "dp", scatter_dimension=0, tiled=True)
        pieces = grads.reshape(half, 2, n_own, piece_rows, width_part).transpose(2, 0, 1, 3, 4)
        pieces = pieces.reshape(n_own, half, 2 * piece_rows * width_part)
        arrived_grad = lax.all_to_all(pieces, "own", split_axis=0, concat_axis=0, tiled=True)
        if h == halves - 1:
            arrived_grad, pred_slots = lax.optimization_barrier((arrived_grad, pred_slots))
            part = sum_by_insertion(item_rows[:, chosen].reshape(-1), arrived_grad, number)
            table = part + table
        else:
            sent = arrived_grad
    pred_slots = pred_slots.astype(jnp.bfloat16)
    table = table.reshape(number, 2, piece_rows, width_part)
    own_params = my_width.astype(jnp.float32)
    fresh_part, new_moment1, new_moment2 = adam_step(own_params, moment1, moment2, table)
    new_weights = lax.all_gather(fresh_part, "dp", axis=0, tiled=False)
    new_weights = new_weights.transpose(1, 2, 3, 0, 4).reshape(weights.shape)
    predicted = pred_slots.reshape(-1, SITES)
    return (predicted, new_weights, new_moment1, new_moment2)


def solution(mesh):
    in_specs = (
        P(("dp", "own"), None),
        P(("dp", "own"), None),
        P(("dp", "own")),
        P(),
        P(),
        P(None, None, "own", None),
        P(None, None, "own", "dp"),
        P(None, None, "own", "dp"),
    )
    out_specs = (
        P(("dp", "own"), None),
        P(None, None, "own", None),
        P(None, None, "own", "dp"),
        P(None, None, "own", "dp"),
    )
    return jax.shard_map(shards, mesh=mesh, in_specs=in_specs, out_specs=out_specs, check_vma=False)
```

```python
import functools
import math

import jax
import jax.numpy as jnp
from jax import lax
from jax.experimental import pallas as pl
from jax.experimental.pallas import tpu as pltpu
from jax.sharding import PartitionSpec as P

SITES = 384
WIDTH = 1024
TOUCH = 4
CAP = 128

MESH = pl.DeviceIdType.MESH

def _a2a_kernel(n_dp, n_own, full, x_ref, o_ref, send_sems, recv_sems, local_sem):
    dp_at = lax.axis_index("dp")
    own_at = lax.axis_index("own")
    if full:
        n = n_dp * n_own
        me = dp_at * n_own + own_at
        def dev(k):
            return (k // n_own, k % n_own)
    else:
        n = n_own
        me = own_at
        def dev(k):
            return (dp_at, k)
    barrier = pltpu.get_barrier_semaphore()

    def greet(i, c):
        peer = lax.rem(me + i, n)
        pl.semaphore_signal(barrier, 1, device_id=dev(peer), device_id_type=MESH)
        return c

    lax.fori_loop(1, n, greet, 0)
    pl.semaphore_wait(barrier, n - 1)
    local = pltpu.make_async_copy(x_ref.at[me], o_ref.at[me], local_sem)
    local.start()

    def send(i, c):
        peer = lax.rem(me + i, n)
        pltpu.make_async_remote_copy(
            src_ref=x_ref.at[peer], dst_ref=o_ref.at[me],
            send_sem=send_sems.at[peer], recv_sem=recv_sems.at[me],
            device_id=dev(peer), device_id_type=MESH,
        ).start()
        return c

    lax.fori_loop(1, n, send, 0)

    def finish(i, c):
        peer = lax.rem(me + i, n)
        src = lax.rem(me + n - i, n)
        pltpu.make_async_remote_copy(
            src_ref=x_ref.at[peer], dst_ref=o_ref.at[src],
            send_sem=send_sems.at[peer], recv_sem=recv_sems.at[src],
            device_id=dev(peer), device_id_type=MESH,
        ).wait_send()
        pltpu.make_async_remote_copy(
            src_ref=x_ref.at[peer], dst_ref=o_ref.at[src],
            send_sem=send_sems.at[peer], recv_sem=recv_sems.at[src],
            device_id=dev(src), device_id_type=MESH,
        ).wait_recv()
        return c

    lax.fori_loop(1, n, finish, 0)
    local.wait()


def exchange(x, n_dp, n_own, full, cid):
    n = x.shape[0]
    return pl.pallas_call(
        functools.partial(_a2a_kernel, n_dp, n_own, full),
        out_shape=jax.ShapeDtypeStruct(x.shape, x.dtype),
        in_specs=[pl.BlockSpec(memory_space=pl.ANY)],
        out_specs=pl.BlockSpec(memory_space=pl.ANY),
        scratch_shapes=[
            pltpu.SemaphoreType.DMA((n,)),
            pltpu.SemaphoreType.DMA((n,)),
            pltpu.SemaphoreType.DMA,
        ],
        compiler_params=pltpu.CompilerParams(collective_id=cid, has_side_effects=True),
    )(x)


gelu_coef = math.sqrt(2.0 / math.pi)
cubic_coef = 0.044715
learn_rate = 0.01
highest = lax.Precision.HIGHEST


def gelu_parts(preact):
    tanh_input = gelu_coef * (preact + cubic_coef * preact * preact * preact)
    tangent = jnp.tanh(tanh_input)
    gelu_val = 0.5 * preact * (1.0 + tangent)
    slopes = 0.5 * (1.0 + tangent) + 0.5 * preact * (1.0 - tangent * tangent) * gelu_coef * (
        1.0 + 3.0 * cubic_coef * preact * preact
    )
    return (gelu_val, slopes)


def dispatch(row_ids, listed):
    match_table = (row_ids[:, None] == listed[None, :]).astype(jnp.int32)
    running = jnp.cumsum(match_table, axis=0) - 1
    slot_of = jnp.sum(match_table * jnp.arange(listed.shape[0], dtype=jnp.int32)[None, :], axis=1)
    within = jnp.sum(match_table * running, axis=1)
    return slot_of * CAP + within


def adam_step(params, moment_one, moment_two, gradient):
    moment_one = 0.9 * moment_one + 0.1 * gradient
    moment_two = 0.999 * moment_two + 0.001 * gradient * gradient
    correct_one = 1.0 - 0.9**10
    correct_two = 1.0 - 0.999**10
    updated = params - learn_rate * (moment_one / correct_one) / (
        jnp.sqrt(moment_two / correct_two) + 1e-08
    )
    return (updated.astype(jnp.bfloat16), moment_one, moment_two)


def sum_by_insertion(item_rows, arrived_grad, number):
    one_hot = (jnp.arange(number, dtype=jnp.int32)[:, None] == item_rows[None, :]).astype(
        arrived_grad.dtype
    )
    flat_grad = arrived_grad.reshape(item_rows.shape[0], -1)
    return jnp.dot(one_hot, flat_grad, preferred_element_type=jnp.float32)


def shards(signals, cotangent, row_insertion, touched, slot_map, weights, moment1, moment2):
    n_own = lax.axis_size("own")
    n_dp = lax.axis_size("dp")
    dp_at = lax.axis_index("dp")
    own_at = lax.axis_index("own")
    number = weights.shape[0]
    piece_rows = weights.shape[2]
    width_part = moment1.shape[3]
    pairs = n_dp * TOUCH
    stored = jnp.sum(
        jnp.where(
            touched[:, :, None] == jnp.arange(number, dtype=jnp.int32)[None, None, :],
            slot_map[None, None, :],
            0,
        ),
        axis=2,
    )
    peer_rows = stored.reshape(n_dp, n_own, TOUCH).transpose(1, 0, 2).reshape(-1)
    my_list = lax.dynamic_index_in_dim(touched, dp_at * n_own + own_at, 0, keepdims=False)
    places = dispatch(row_insertion, my_list)
    stacked = (
        jnp.zeros((TOUCH * CAP, 2 * SITES), signals.dtype)
        .at[places]
        .set(jnp.concatenate([signals, cotangent], axis=1))
    )
    stacked = lax.all_gather(stacked.reshape(TOUCH, CAP, 2 * SITES), "dp", axis=0, tiled=True)
    stacked = stacked.reshape(pairs, CAP, 2 * SITES)
    sig_slots = stacked[:, :, :SITES]
    cot_slots = stacked[:, :, SITES:]
    my_width = lax.dynamic_slice_in_dim(weights, dp_at * width_part, width_part, 3)
    pick = (peer_rows[:, None] == jnp.arange(number, dtype=jnp.int32)[None, :]).astype(weights.dtype)
    outgoing = jnp.dot(
        pick, my_width.reshape(number, -1), preferred_element_type=jnp.float32
    ).astype(weights.dtype)
    outgoing = outgoing.reshape(n_own, pairs, 2 * piece_rows * width_part)
    item_rows = peer_rows.reshape(n_own, pairs)
    halves = 2
    half = pairs // halves
    pred_parts = []
    table = None
    fetched = [
        lax.all_to_all(
            outgoing[:, h * half : (h + 1) * half], "own", split_axis=0, concat_axis=0, tiled=True
        )
        for h in range(halves)
    ]
    sent = None
    for h in range(halves):
        chosen = slice(h * half, (h + 1) * half)
        arrived = fetched[h]
        arrived = arrived.reshape(n_own, half, 2, piece_rows, width_part)
        arrived = arrived.transpose(1, 2, 0, 3, 4).reshape(half, 2, SITES, width_part)
        read_in = arrived[:, 0]
        read_out = arrived[:, 1]
        sig_part = sig_slots[chosen]
        cot_part = cot_slots[chosen]
        preact = jnp.einsum("kcs,ksw->kcw", sig_part, read_in, preferred_element_type=jnp.float32)
        gelu_val, slopes = gelu_parts(preact)
        hidden = gelu_val.astype(jnp.bfloat16)
        pred_parts.append(
            jnp.einsum("kcw,ksw->kcs", hidden, read_out, preferred_element_type=jnp.float32)
        )
        back_hidden = jnp.einsum(
            "kcs,ksw->kcw", cot_part, read_out, preferred_element_type=jnp.float32
        )
        back_pre = (back_hidden * slopes).astype(jnp.bfloat16)
        grad_in = jnp.einsum("kcs,kcw->ksw", sig_part, back_pre, preferred_element_type=jnp.float32)
        grad_out = jnp.einsum("kcs,kcw->ksw", cot_part, hidden, preferred_element_type=jnp.float32)
        grads = jnp.stack([grad_in, grad_out], axis=1).astype(jnp.bfloat16)
        if h + 1 < halves:
            grads, fetched[h + 1] = lax.optimization_barrier((grads, fetched[h + 1]))
        if sent is not None:
            grads, sent = lax.optimization_barrier((grads, sent))
            table = sum_by_insertion(item_rows[:, :half].reshape(-1), sent, number)
        if h == halves - 1:
            pred_part = jnp.concatenate(pred_parts, axis=0)
            pred_part, grads = lax.optimization_barrier((pred_part, grads))
            pred_slots = lax.psum_scatter(pred_part, "dp", scatter_dimension=0, tiled=True)
        pieces = grads.reshape(half, 2, n_own, piece_rows, width_part).transpose(2, 0, 1, 3, 4)
        pieces = pieces.reshape(n_own, half, 2 * piece_rows * width_part)
        arrived_grad = lax.all_to_all(pieces, "own", split_axis=0, concat_axis=0, tiled=True)
        if h == halves - 1:
            arrived_grad, pred_slots = lax.optimization_barrier((arrived_grad, pred_slots))
            part = sum_by_insertion(item_rows[:, chosen].reshape(-1), arrived_grad, number)
            table = part + table
        else:
            sent = arrived_grad
    pred_slots = pred_slots.astype(jnp.bfloat16)
    table = table.reshape(number, 2, piece_rows, width_part)
    own_params = my_width.astype(jnp.float32)
    fresh_part, new_moment1, new_moment2 = adam_step(own_params, moment1, moment2, table)
    new_weights = lax.all_gather(fresh_part.reshape(-1, width_part), "dp", axis=0, tiled=False)
    new_weights = new_weights.transpose(1, 0, 2).reshape(weights.shape)
    predicted = pred_slots.reshape(TOUCH * CAP, SITES)[places]
    return (predicted, new_weights, new_moment1, new_moment2)


def solution(mesh):
    in_specs = (
        P(("dp", "own"), None),
        P(("dp", "own"), None),
        P(("dp", "own")),
        P(),
        P(),
        P(None, None, "own", None),
        P(None, None, "own", "dp"),
        P(None, None, "own", "dp"),
    )
    out_specs = (
        P(("dp", "own"), None),
        P(None, None, "own", None),
        P(None, None, "own", "dp"),
        P(None, None, "own", "dp"),
    )
    return jax.shard_map(shards, mesh=mesh, in_specs=in_specs, out_specs=out_specs, check_vma=False)
```

```python
import functools
import math

import jax
import jax.numpy as jnp
from jax import lax
from jax.experimental import pallas as pl
from jax.experimental.pallas import tpu as pltpu
from jax.sharding import PartitionSpec as P

SITES = 384
WIDTH = 1024
TOUCH = 4
CAP = 128

MESH = pl.DeviceIdType.MESH

def _a2a_kernel(n_dp, n_own, full, x_ref, o_ref, send_sems, recv_sems, local_sem):
    dp_at = lax.axis_index("dp")
    own_at = lax.axis_index("own")
    if full:
        n = n_dp * n_own
        me = dp_at * n_own + own_at
        def dev(k):
            return (k // n_own, k % n_own)
    else:
        n = n_own
        me = own_at
        def dev(k):
            return (dp_at, k)
    barrier = pltpu.get_barrier_semaphore()

    def greet(i, c):
        peer = lax.rem(me + i, n)
        pl.semaphore_signal(barrier, 1, device_id=dev(peer), device_id_type=MESH)
        return c

    lax.fori_loop(1, n, greet, 0)
    pl.semaphore_wait(barrier, n - 1)
    local = pltpu.make_async_copy(x_ref.at[me], o_ref.at[me], local_sem)
    local.start()

    def send(i, c):
        peer = lax.rem(me + i, n)
        pltpu.make_async_remote_copy(
            src_ref=x_ref.at[peer], dst_ref=o_ref.at[me],
            send_sem=send_sems.at[peer], recv_sem=recv_sems.at[me],
            device_id=dev(peer), device_id_type=MESH,
        ).start()
        return c

    lax.fori_loop(1, n, send, 0)

    def finish(i, c):
        peer = lax.rem(me + i, n)
        src = lax.rem(me + n - i, n)
        pltpu.make_async_remote_copy(
            src_ref=x_ref.at[peer], dst_ref=o_ref.at[src],
            send_sem=send_sems.at[peer], recv_sem=recv_sems.at[src],
            device_id=dev(peer), device_id_type=MESH,
        ).wait_send()
        pltpu.make_async_remote_copy(
            src_ref=x_ref.at[peer], dst_ref=o_ref.at[src],
            send_sem=send_sems.at[peer], recv_sem=recv_sems.at[src],
            device_id=dev(src), device_id_type=MESH,
        ).wait_recv()
        return c

    lax.fori_loop(1, n, finish, 0)
    local.wait()


def exchange(x, n_dp, n_own, full, cid):
    n = x.shape[0]
    return pl.pallas_call(
        functools.partial(_a2a_kernel, n_dp, n_own, full),
        out_shape=jax.ShapeDtypeStruct(x.shape, x.dtype),
        in_specs=[pl.BlockSpec(memory_space=pl.ANY)],
        out_specs=pl.BlockSpec(memory_space=pl.ANY),
        scratch_shapes=[
            pltpu.SemaphoreType.DMA((n,)),
            pltpu.SemaphoreType.DMA((n,)),
            pltpu.SemaphoreType.DMA,
        ],
        compiler_params=pltpu.CompilerParams(collective_id=cid, has_side_effects=True),
    )(x)


gelu_coef = math.sqrt(2.0 / math.pi)
cubic_coef = 0.044715
learn_rate = 0.01
highest = lax.Precision.HIGHEST


def gelu_parts(preact):
    tanh_input = gelu_coef * (preact + cubic_coef * preact * preact * preact)
    tangent = jnp.tanh(tanh_input)
    gelu_val = 0.5 * preact * (1.0 + tangent)
    slopes = 0.5 * (1.0 + tangent) + 0.5 * preact * (1.0 - tangent * tangent) * gelu_coef * (
        1.0 + 3.0 * cubic_coef * preact * preact
    )
    return (gelu_val, slopes)


def dispatch(row_ids, listed):
    match_table = (row_ids[:, None] == listed[None, :]).astype(jnp.int32)
    running = jnp.cumsum(match_table, axis=0) - 1
    slot_of = jnp.sum(match_table * jnp.arange(listed.shape[0], dtype=jnp.int32)[None, :], axis=1)
    within = jnp.sum(match_table * running, axis=1)
    return slot_of * CAP + within


def adam_step(params, moment_one, moment_two, gradient):
    moment_one = 0.9 * moment_one + 0.1 * gradient
    moment_two = 0.999 * moment_two + 0.001 * gradient * gradient
    correct_one = 1.0 - 0.9**10
    correct_two = 1.0 - 0.999**10
    updated = params - learn_rate * (moment_one / correct_one) / (
        jnp.sqrt(moment_two / correct_two) + 1e-08
    )
    return (updated.astype(jnp.bfloat16), moment_one, moment_two)


def sum_by_insertion(item_rows, arrived_grad, number):
    one_hot = (jnp.arange(number, dtype=jnp.int32)[:, None] == item_rows[None, :]).astype(
        arrived_grad.dtype
    )
    flat_grad = arrived_grad.reshape(item_rows.shape[0], -1)
    return jnp.dot(one_hot, flat_grad, preferred_element_type=jnp.float32)


def shards(signals, cotangent, row_insertion, touched, slot_map, weights, moment1, moment2):
    n_own = lax.axis_size("own")
    n_dp = lax.axis_size("dp")
    dp_at = lax.axis_index("dp")
    own_at = lax.axis_index("own")
    number = weights.shape[0]
    piece_rows = weights.shape[2]
    width_part = moment1.shape[3]
    pairs = n_dp * TOUCH
    stored = jnp.sum(
        jnp.where(
            touched[:, :, None] == jnp.arange(number, dtype=jnp.int32)[None, None, :],
            slot_map[None, None, :],
            0,
        ),
        axis=2,
    )
    peer_rows = stored.reshape(n_dp, n_own, TOUCH).transpose(1, 0, 2).reshape(-1)
    my_list = lax.dynamic_index_in_dim(touched, dp_at * n_own + own_at, 0, keepdims=False)
    places = dispatch(row_insertion, my_list)
    row_of_slot = (
        jnp.full((TOUCH * CAP,), -1, jnp.int32)
        .at[places]
        .set(jnp.arange(places.shape[0], dtype=jnp.int32))
        .astype(signals.dtype)
    )
    stacked = (
        jnp.zeros((TOUCH * CAP, 2 * SITES), signals.dtype)
        .at[places]
        .set(jnp.concatenate([signals, cotangent], axis=1))
    )
    extra = jnp.zeros((16, 2 * SITES), signals.dtype).at[0, : TOUCH * CAP].set(row_of_slot)
    gathered = lax.all_gather(
        jnp.concatenate([stacked, extra], axis=0), "dp", axis=0, tiled=False
    )
    stacked = gathered[:, : TOUCH * CAP]
    peer_slots = gathered[:, TOUCH * CAP, : TOUCH * CAP].astype(jnp.int32)
    stacked = stacked.reshape(pairs, CAP, 2 * SITES)
    sig_slots = stacked[:, :, :SITES]
    cot_slots = stacked[:, :, SITES:]
    my_width = lax.dynamic_slice_in_dim(weights, dp_at * width_part, width_part, 3)
    pick = (peer_rows[:, None] == jnp.arange(number, dtype=jnp.int32)[None, :]).astype(weights.dtype)
    outgoing = jnp.dot(
        pick, my_width.reshape(number, -1), preferred_element_type=jnp.float32
    ).astype(weights.dtype)
    outgoing = outgoing.reshape(n_own, pairs, 2 * piece_rows * width_part)
    item_rows = peer_rows.reshape(n_own, pairs)
    halves = 2
    half = pairs // halves
    pred_parts = []
    table = None
    fetched = [
        lax.all_to_all(
            outgoing[:, h * half : (h + 1) * half], "own", split_axis=0, concat_axis=0, tiled=True
        )
        for h in range(halves)
    ]
    sent = None
    for h in range(halves):
        chosen = slice(h * half, (h + 1) * half)
        arrived = fetched[h]
        arrived = arrived.reshape(n_own, half, 2, piece_rows, width_part)
        arrived = arrived.transpose(1, 2, 0, 3, 4).reshape(half, 2, SITES, width_part)
        read_in = arrived[:, 0]
        read_out = arrived[:, 1]
        sig_part = sig_slots[chosen]
        cot_part = cot_slots[chosen]
        preact = jnp.einsum("kcs,ksw->kcw", sig_part, read_in, preferred_element_type=jnp.float32)
        gelu_val, slopes = gelu_parts(preact)
        hidden = gelu_val.astype(jnp.bfloat16)
        pred_parts.append(
            jnp.einsum("kcw,ksw->kcs", hidden, read_out, preferred_element_type=jnp.float32)
        )
        back_hidden = jnp.einsum(
            "kcs,ksw->kcw", cot_part, read_out, preferred_element_type=jnp.float32
        )
        back_pre = (back_hidden * slopes).astype(jnp.bfloat16)
        grad_in = jnp.einsum("kcs,kcw->ksw", sig_part, back_pre, preferred_element_type=jnp.float32)
        grad_out = jnp.einsum("kcs,kcw->ksw", cot_part, hidden, preferred_element_type=jnp.float32)
        grads = jnp.stack([grad_in, grad_out], axis=1).astype(jnp.bfloat16)
        if h + 1 < halves:
            grads, fetched[h + 1] = lax.optimization_barrier((grads, fetched[h + 1]))
        if sent is not None:
            grads, sent = lax.optimization_barrier((grads, sent))
            table = sum_by_insertion(item_rows[:, :half].reshape(-1), sent, number)
        if h == halves - 1:
            pred_part = jnp.concatenate(pred_parts, axis=0)
            pred_part, grads = lax.optimization_barrier((pred_part, grads))
            pred_part = pred_part.reshape(n_dp, TOUCH * CAP, SITES)
            choose = (
                peer_slots[:, None, :]
                == jnp.arange(signals.shape[0], dtype=jnp.int32)[None, :, None]
            ).astype(jnp.float32)
            real_rows = jnp.einsum(
                "qrs,qsx->qrx", choose, pred_part, precision=lax.Precision.HIGH,
                preferred_element_type=jnp.float32,
            )
            pred_slots = lax.psum_scatter(real_rows, "dp", scatter_dimension=0, tiled=True)
        pieces = grads.reshape(half, 2, n_own, piece_rows, width_part).transpose(2, 0, 1, 3, 4)
        pieces = pieces.reshape(n_own, half, 2 * piece_rows * width_part)
        arrived_grad = lax.all_to_all(pieces, "own", split_axis=0, concat_axis=0, tiled=True)
        if h == halves - 1:
            arrived_grad, pred_slots = lax.optimization_barrier((arrived_grad, pred_slots))
            part = sum_by_insertion(item_rows[:, chosen].reshape(-1), arrived_grad, number)
            table = part + table
        else:
            sent = arrived_grad
    pred_slots = pred_slots.astype(jnp.bfloat16)
    table = table.reshape(number, 2, piece_rows, width_part)
    own_params = my_width.astype(jnp.float32)
    fresh_part, new_moment1, new_moment2 = adam_step(own_params, moment1, moment2, table)
    new_weights = lax.all_gather(fresh_part, "dp", axis=0, tiled=False)
    new_weights = new_weights.transpose(1, 2, 3, 0, 4).reshape(weights.shape)
    predicted = pred_slots.reshape(-1, SITES)
    return (predicted, new_weights, new_moment1, new_moment2)


def solution(mesh):
    in_specs = (
        P(("dp", "own"), None),
        P(("dp", "own"), None),
        P(("dp", "own")),
        P(),
        P(),
        P(None, None, "own", None),
        P(None, None, "own", "dp"),
        P(None, None, "own", "dp"),
    )
    out_specs = (
        P(("dp", "own"), None),
        P(None, None, "own", None),
        P(None, None, "own", "dp"),
        P(None, None, "own", "dp"),
    )
    return jax.shard_map(shards, mesh=mesh, in_specs=in_specs, out_specs=out_specs, check_vma=False)
```
